32 devices in a mesh: dev: 32 (over z, y, x, core).
Axes of the slice: x: 2, y: 2, z: 4, core: 2. Of those that a mesh axis runs over, the one named last changes fastest.
Arguments:
- right_side: float32 [2048, 3, 128], P('dev'), may hold values from -105 to 105
- vertices: float32 [2048, 3, 128], P('dev'), may hold values from 0 to 1
- panels: int32 [2048, 3, 128], P('dev'), may hold values from 0 to 127
- near_owner: int32 [2048, 2], P('dev'), may hold values from 0 to 31, all different within a row; in each aligned block of 64 rows (0 to 63, 64 to 127, ...) at most 8 rows name the same one
- near_local: int32 [2048, 2], P('dev'), may hold values from 0 to 63
- far_owner: int32 [2048, 2], P('dev'), may hold values from 0 to 31, all different within a row; in each aligned block of 64 rows (0 to 63, 64 to 127, ...) at most 8 rows name the same one
- far_local: int32 [2048, 2], P('dev'), may hold values from 0 to 63
- far_left: float32 [2048, 16, 384], P('dev'), may hold values from -0.5 to 0.5
- far_right: float32 [2048, 16, 384], P('dev'), may hold values from -0.5 to 0.5
Outputs:
- krylov_basis: float32 [2, 2048, 3, 128], P(None, 'dev')
- hessenberg: float32 [3, 2], replicated
The draws below stay inside these ranges and needn't reach their ends.
Inputs may be any that keep to these rules, and one draw needn't show every extreme that they name: `near_owner`: the two entries of a row differ. Within one device's 64 rows no device number appears more than 8 times, and in every draw some number appears exactly 8 times. `far_owner`: the two entries of a row differ. Within one device's 64 rows no device number appears more than 8 times, and in every draw some number appears exactly 8 times.
All inputs are finite; a program needn't handle non-finite values.
Results may differ from the reference program's by a relative error of at most 0.0003.
Values sent between devices are 32-bit elements; how exact they have to be, the bound alone decides.
No kernel may reach another device: no remote copies, remote signals or barrier semaphores. Data moves between devices by JAX's collectives and lax.ppermute only.
A program may use at most 64 MiB of HBM per device.

```python
import math
import jax
import jax.numpy as jnp
import numpy as np
from jax import lax

P_SIZE = 128
NV = 128
R = 16
CL_DEV = 64
NEAR_DEV = 64
FAR_DEV = 64
CAP_NEAR = 8
CAP_FAR = 8
CLUSTERS = 2048
NEAR = 2048
FAR = 2048
N_DEV = 32


def draw_right_side(key, part):
    key_value, key_row, key_col = jax.random.split(key, 3)
    position = jnp.arange(CLUSTERS, dtype=jnp.float32).reshape(CLUSTERS, 1, 1) / CLUSTERS
    row_scale = jnp.exp(jax.random.uniform(key_row, (CLUSTERS, 1, 1), jnp.float32) * math.log(10.0))
    col_scale = jnp.exp(jax.random.uniform(key_col, (1, 1, P_SIZE), jnp.float32) * math.log(10.0))
    values = jnp.clip(jax.random.normal(key_value, (CLUSTERS, 3, P_SIZE), jnp.float32), -6.0, 6.0)
    rising = 1.0 + 0.75 * position
    return values * row_scale * col_scale * rising / 10.0


def plant(entries, own_key, low, largest):
    longest = entries.shape.index(max(entries.shape))
    spots = []
    for shift in (0, 1):
        where = [jax.random.randint(jax.random.fold_in(own_key, axis), (), 0, length) for axis, length in enumerate(entries.shape)]
        where[longest] = (where[longest] + shift) % entries.shape[longest]
        spots.append(tuple(where))
    return entries.at[spots[0]].set(low).at[spots[1]].set(largest)


def block_levels(key, extent, shards, low, largest):
    def one(dim, shards_of):
        steps = jax.random.uniform(jax.random.fold_in(jax.random.fold_in(key, 6), dim), (shards_of,), jnp.float32, low / len(shards), largest / len(shards))
        return jnp.repeat(jnp.exp(steps), extent[dim] // shards_of).reshape((-1,) + (1,) * (len(extent) - dim - 1))

    loudness = one(*shards[0])
    for cut in shards[1:]:
        loudness = loudness * one(*cut)
    return loudness


def assign_block(own_key, own, number, rows, count, top, limit, skew):
    ranking = jax.random.permutation(own_key, count)
    packed, usual = shares(count, rows * top, limit, skew, True), shares(count, rows * top, limit, skew, False)
    places = jnp.arange(count)

    def named(tallies, turn):
        used = int((tallies > 0).sum())
        fixed = max(1, used // 4)
        shifted = fixed + (places - fixed + turn * (used - fixed)) % max(1, count - fixed)
        return jnp.zeros((count,), jnp.int32).at[ranking[jnp.where(places < fixed, places, shifted)]].set(jnp.asarray(tallies, jnp.int32))

    tallies = jnp.where(number % 4 == 0, named(packed, number // 4), named(usual, number - number // 4 - 1))
    mixed = jax.random.permutation(jax.random.fold_in(own, 3), count)
    donor, sink = mixed[0:count // 2 * 2:2], mixed[1:count // 2 * 2:2]
    slack = jnp.minimum(tallies[donor] - 1, limit - tallies[sink]) // 2
    slack = jnp.where((donor == ranking[0]) | (sink == ranking[0]) | (tallies[sink] == 0), 0, jnp.maximum(slack, 0))
    shifted = jax.random.randint(jax.random.fold_in(own, 4), (count // 2,), 0, 1 << 20) % (slack + 1)
    tallies = tallies.at[donor].add(-shifted).at[sink].add(shifted)
    members = jnp.searchsorted(jnp.cumsum(tallies), jnp.arange(rows * top), side="right").astype(jnp.int32)
    table = members.reshape(top, rows).T
    table = table[jax.random.permutation(jax.random.fold_in(own, 1), rows)]
    turn = jax.random.randint(jax.random.fold_in(own, 2), (rows, 1), 0, top)
    return jnp.take_along_axis(table, (jnp.arange(top)[None, :] + turn) % top, axis=1)


def shares(number_of, total, limit, slope, full):
    weights = [(1 << 20) // math.isqrt(standing ** slope) + 1 for standing in range(1, number_of + 1)]
    largest = limit if full else min(limit, max(-(-total // number_of), total * weights[0] // sum(weights)))
    least = 1 if total - largest >= number_of - 1 else 0
    given, spare = [largest] + [least] * (number_of - 1), total - largest - least * (number_of - 1)
    while spare > 0:
        candidates = [i for i in range(1, number_of) if given[i] < largest] or [i for i in range(1, number_of) if given[i] < limit]
        mass, left = sum([weights[i] for i in candidates]), spare
        for i in candidates:
            extra = min(limit - given[i], max(1, left * weights[i] // mass), spare)
            given[i] = given[i] + extra
            spare = spare - extra
    return np.array(given)


def bell_draw(key, dims, deviation, reach, cuts=(), held_as=jnp.bfloat16):
    loudness = block_levels(key, dims, cuts, -0.22, 0.18) if cuts else 1.0
    drawn = jax.random.normal(key, dims, jnp.float32) * deviation * loudness
    return jnp.minimum(jnp.maximum(drawn, -reach), reach).astype(held_as)


def setup_inputs(seed: int = 0) -> dict:
    seeds = jax.random.split(jax.random.key(seed), 10)
    right_side = draw_right_side(jax.random.fold_in(seeds[9], 71), 0)
    vertices = jnp.clip(1.0 * jax.random.uniform(seeds[1], (CLUSTERS, 3, NV), jnp.float32) ** block_levels(seeds[1], (CLUSTERS, 3, NV), ((0, 32),), -0.2, 0.2), 0.0, 1.0)
    panels = plant(jax.random.randint(seeds[2], (CLUSTERS, 3, P_SIZE), 0, NV), jax.random.fold_in(seeds[2], 1), 0, NV - 1).astype(jnp.int32)
    near_owner_keys = jax.random.split(jax.random.fold_in(seeds[3], 1), NEAR // NEAR_DEV)
    near_owner_turns = jax.random.permutation(jax.random.fold_in(seeds[3], 3), NEAR // NEAR_DEV)
    near_owner = jax.vmap(lambda own, number: assign_block(jax.random.fold_in(seeds[3], 2), own, number, NEAR_DEV, N_DEV, 2, CAP_NEAR, 2))(near_owner_keys, near_owner_turns).reshape((NEAR, 2))
    near_local = plant(jax.random.randint(seeds[4], (NEAR, 2), 0, CL_DEV), jax.random.fold_in(seeds[4], 1), 0, CL_DEV - 1).astype(jnp.int32)
    far_owner_keys = jax.random.split(jax.random.fold_in(seeds[5], 1), FAR // FAR_DEV)
    far_owner_turns = jax.random.permutation(jax.random.fold_in(seeds[5], 3), FAR // FAR_DEV)
    far_owner = jax.vmap(lambda own, number: assign_block(jax.random.fold_in(seeds[5], 2), own, number, FAR_DEV, N_DEV, 2, CAP_FAR, 2))(far_owner_keys, far_owner_turns).reshape((FAR, 2))
    far_local = plant(jax.random.randint(seeds[6], (FAR, 2), 0, CL_DEV), jax.random.fold_in(seeds[6], 1), 0, CL_DEV - 1).astype(jnp.int32)
    far_left = bell_draw(seeds[7], (FAR, R, 3 * P_SIZE), P_SIZE ** -0.5, 0.5, ((0, 32),), jnp.float32)
    far_right = bell_draw(seeds[8], (FAR, R, 3 * P_SIZE), P_SIZE ** -0.5, 0.5, ((0, 32),), jnp.float32)
    return {"right_side": right_side, "vertices": vertices, "panels": panels, "near_owner": near_owner, "near_local": near_local, "far_owner": far_owner, "far_local": far_local, "far_left": far_left, "far_right": far_right}


highest = lax.Precision.HIGHEST
soft_sq = 0.0025
area_floor = 6.25e-06
kelvin_diag = 1.8
norm_eps = 1e-06
barycentric = ((2.0 / 3.0, 1.0 / 6.0, 1.0 / 6.0), (1.0 / 6.0, 2.0 / 3.0, 1.0 / 6.0), (1.0 / 6.0, 1.0 / 6.0, 2.0 / 3.0))
index_pairs = ((0, 0), (0, 1), (0, 2), (1, 1), (1, 2), (2, 2))

def panel_corners(vertex_table, connect):
    return jnp.stack([jnp.take(vertex_table, connect[m], axis=1) for m in range(3)])

def quad_points(corners):
    edge_one = corners[1] - corners[0]
    edge_two = corners[2] - corners[0]
    cross_x = edge_one[1] * edge_two[2] - edge_one[2] * edge_two[1]
    cross_y = edge_one[2] * edge_two[0] - edge_one[0] * edge_two[2]
    cross_z = edge_one[0] * edge_two[1] - edge_one[1] * edge_two[0]
    weight = jnp.sqrt(cross_x * cross_x + cross_y * cross_y + cross_z * cross_z + area_floor) / 6.0
    points = jnp.stack([coords[0] * corners[0] + coords[1] * corners[1] + coords[2] * corners[2] for coords in barycentric])
    return (points, weight)

def near_block(points_first, weight_first, points_second, weight_second):
    panel_count = weight_first.shape[0]
    diag_sum = jnp.zeros((panel_count, panel_count), jnp.float32)
    outer_terms = [jnp.zeros((panel_count, panel_count), jnp.float32) for pair_index in index_pairs]
    for s in range(3):
        for t in range(3):
            offset = points_first[s][:, :, None] - points_second[t][:, None, :]
            inverse = lax.rsqrt(offset[0] * offset[0] + offset[1] * offset[1] + offset[2] * offset[2] + soft_sq)
            diag_sum = diag_sum + inverse
            inverse_cube = inverse * inverse * inverse
            outer_terms = [partial_sum + inverse_cube * offset[i] * offset[j] for partial_sum, (i, j) in zip(outer_terms, index_pairs)]
    weight_pair = weight_first[:, None] * weight_second[None, :]
    matrix_rows = []
    for i in range(3):
        matrix_row = []
        for j in range(3):
            entry_sum = outer_terms[index_pairs.index((min(i, j), max(i, j)))]
            if i == j:
                entry_sum = entry_sum + kelvin_diag * diag_sum
            matrix_row.append(weight_pair * entry_sum)
        matrix_rows.append(jnp.stack(matrix_row))
    return jnp.stack(matrix_rows)

def apply_near(block_matrix, dense_first, dense_second):
    into_first = jnp.einsum('ijkl,jl->ik', block_matrix, dense_second, precision=highest)
    into_second = jnp.einsum('ijkl,ik->jl', block_matrix, dense_first, precision=highest)
    return (into_first, into_second)

def apply_far(left_factors, right_factors, flat_first, flat_second):
    coef_second = jnp.einsum('frk,fk->fr', right_factors, flat_second, precision=highest)
    into_first = jnp.einsum('frk,fr->fk', left_factors, coef_second, precision=highest)
    coef_first = jnp.einsum('frk,fk->fr', left_factors, flat_first, precision=highest)
    into_second = jnp.einsum('frk,fr->fk', right_factors, coef_first, precision=highest)
    return (into_first, into_second)

def reference(right_side, vertices, panels, near_owner, near_local, far_owner, far_local, far_left, far_right):
    corners = jax.vmap(panel_corners)(vertices, panels)
    points, weights = jax.vmap(quad_points)(corners)
    near_ids = (near_owner * CL_DEV + near_local).astype(jnp.int32)
    far_ids = (far_owner * CL_DEV + far_local).astype(jnp.int32)
    size_all = CLUSTERS * 3 * P_SIZE

    def product(density):

        def near_step(image_sum, pair_ids):
            ids_first = pair_ids[:, 0]
            ids_second = pair_ids[:, 1]
            blocks = jax.vmap(near_block)(points[ids_first], weights[ids_first], points[ids_second], weights[ids_second])
            into_first, into_second = jax.vmap(apply_near)(blocks, density[ids_first], density[ids_second])
            image_sum = image_sum.at[ids_first].add(into_first).at[ids_second].add(into_second)
            return (image_sum, None)
        image_sum, unused_out = lax.scan(near_step, jnp.zeros((CLUSTERS, 3, P_SIZE), jnp.float32), near_ids.reshape(N_DEV * NEAR_DEV // 4, 4, 2))
        flat_density = density.reshape(CLUSTERS, 3 * P_SIZE)
        far_first, far_second = apply_far(far_left, far_right, flat_density[far_ids[:, 0]], flat_density[far_ids[:, 1]])
        image_sum = image_sum.reshape(CLUSTERS, 3 * P_SIZE).at[far_ids[:, 0]].add(far_first).at[far_ids[:, 1]].add(far_second)
        return image_sum.reshape(CLUSTERS, 3, P_SIZE)

    def mean_inner(left_vec, right_vec):
        return jnp.sum(left_vec * right_vec) / size_all
    rhs_scale = jnp.sqrt(mean_inner(right_side, right_side) + norm_eps)
    basis_one = right_side / rhs_scale
    image_one = product(basis_one)
    proj_first = mean_inner(basis_one, image_one)
    resid_one = image_one - proj_first * basis_one
    norm_first = jnp.sqrt(mean_inner(resid_one, resid_one) + norm_eps)
    basis_two = resid_one / norm_first
    image_two = product(basis_two)
    proj_cross = mean_inner(basis_one, image_two)
    proj_second = mean_inner(basis_two, image_two)
    resid_two = image_two - proj_cross * basis_one - proj_second * basis_two
    norm_second = jnp.sqrt(mean_inner(resid_two, resid_two) + norm_eps)
    basis_three = resid_two / norm_second
    zero_entry = jnp.zeros((), jnp.float32)
    hessenberg = jnp.stack([jnp.stack([proj_first, proj_cross]), jnp.stack([norm_first, proj_second]), jnp.stack([zero_entry, norm_second])])
    return (jnp.stack([basis_two, basis_three]), hessenberg)
```

```python
import jax
import jax.numpy as jnp
from jax import lax
from jax.experimental import pallas as pl
from jax.experimental.pallas import tpu as pltpu
from jax.sharding import PartitionSpec as P

soft_sq = 0.0025
area_floor = 6.25e-06
kelvin_diag = 1.8
norm_eps = 1e-06
big = 2.0 / 3.0
small = 1.0 / 6.0
COMPS = 16
f32 = jnp.float32
VM = pl.BlockSpec(memory_space=pltpu.VMEM)
SM = pl.BlockSpec(memory_space=pltpu.SMEM)


def params(**kw):
    return pltpu.CompilerParams(vmem_limit_bytes=60 << 20, **kw)


def two_sum(a, b):
    s = a + b
    t = s - a
    return s, (a - (s - t)) + (b - t)


def split(a):
    c = a * 4097.0
    hi = c - (c - a)
    return hi, a - hi


def two_prod(a, b):
    p = a * b
    ah, al = split(a)
    bh, bl = split(b)
    return p, ((ah * bh - p) + ah * bl + al * bh) + al * bl


def dd_add(x, y):
    s, e = two_sum(x[0], y[0])
    e = e + (x[1] + y[1])
    hi = s + e
    return hi, e - (hi - s)


def dd_scale(x, f):
    p, e = two_prod(x[0], f)
    e = e + x[1] * f
    hi = p + e
    return hi, e - (hi - p)


def dd_neg(x):
    return -x[0], -x[1]


def prep_kernel(no_ref, nl_ref, fo_ref, fl_ref, ask_ref, idx_ref, *, cap, trash):
    n = ask_ref.shape[0]
    width = 2 * no_ref.shape[1]
    ask = jnp.full(ask_ref.shape, float(trash), f32)
    rows = []
    for part, (o_ref, l_ref) in enumerate(((no_ref, nl_ref), (fo_ref, fl_ref))):
        owner = jnp.concatenate([o_ref[0:1, :], o_ref[1:2, :]], axis=1).astype(f32)
        local = jnp.concatenate([l_ref[0:1, :], l_ref[1:2, :]], axis=1).astype(f32)
        across = jnp.broadcast_to(owner, (width, width))
        down = across.T
        row = lax.broadcasted_iota(jnp.int32, (width, width), 0)
        col = lax.broadcasted_iota(jnp.int32, (width, width), 1)
        earlier = jnp.where((across == down) & (row < col), 1.0, 0.0)
        rank = jnp.sum(earlier, axis=0, keepdims=True)
        dest = lax.broadcasted_iota(jnp.int32, (n, width), 0).astype(f32)
        lhs = jnp.where(dest == owner, local + 1.0, 0.0).astype(jnp.bfloat16)
        slot = lax.broadcasted_iota(jnp.int32, (ask_ref.shape[1], width), 0).astype(f32)
        rhs = jnp.where(slot == rank + float(part * cap), 1.0, 0.0).astype(jnp.bfloat16)
        found = lax.dot_general(
            lhs, rhs, (((1,), (1,)), ((), ())), preferred_element_type=f32
        )
        ask = jnp.where(found > 0.5, found - 1.0, ask)
        rows += [owner, rank]
    ask_ref[...] = ask.astype(jnp.int32)
    idx_ref[...] = jnp.concatenate(rows + rows, axis=0).astype(jnp.int32)


def pack_kernel(ask_ref, x_ref, v_ref, p_ref, near_ref, far_ref, pan_ref, *, cap):
    n = near_ref.shape[0]
    last = x_ref.shape[1] - 1
    pan_ref[...] = p_ref[...].astype(f32)

    def body(d, _):
        for s in range(cap):
            c = jnp.minimum(ask_ref[d, cap + s], last)
            for i in range(3):
                far_ref[d, i, pl.ds(s, 1), :] = x_ref[i, pl.ds(c, 1), :]
        for s in range(cap):
            c = jnp.minimum(ask_ref[d, s], last)
            for i in range(3):
                near_ref[d, i, pl.ds(s, 1), :] = v_ref[i, pl.ds(c, 1), :]
                near_ref[d, 3 + i, pl.ds(s, 1), :] = pan_ref[i, pl.ds(c, 1), :]
                near_ref[d, 6 + i, pl.ds(s, 1), :] = x_ref[i, pl.ds(c, 1), :]
        return 0

    lax.fori_loop(0, n, body, 0)


def far_kernel(idx_ref, x_ref, l_ref, r_ref, out_ref):
    count = l_ref.shape[0]

    def body(f, _):
        oa, ra = idx_ref[2, f], idx_ref[3, f]
        ob, rb = idx_ref[2, count + f], idx_ref[3, count + f]
        left = [l_ref[f, :, pl.ds(128 * i, 128)] for i in range(3)]
        right = [r_ref[f, :, pl.ds(128 * i, 128)] for i in range(3)]
        xa = [x_ref[oa, i, pl.ds(ra, 1), :] for i in range(3)]
        xb = [x_ref[ob, i, pl.ds(rb, 1), :] for i in range(3)]
        coef_b = jnp.sum(sum(right[i] * xb[i] for i in range(3)), axis=1, keepdims=True)
        coef_a = jnp.sum(sum(left[i] * xa[i] for i in range(3)), axis=1, keepdims=True)
        for i in range(3):
            out_ref[oa, i, pl.ds(ra, 1), :] = jnp.sum(left[i] * coef_b, axis=0, keepdims=True)
            out_ref[ob, i, pl.ds(rb, 1), :] = jnp.sum(right[i] * coef_a, axis=0, keepdims=True)
        return 0

    lax.fori_loop(0, count, body, 0, unroll=4)


def slot_geometry(in_ref, geo_ref, *, cap):
    n = in_ref.shape[0]

    def body(d, _):
        corner = []
        for m in range(3):
            pick = in_ref[d, 3 + m].astype(jnp.int32)
            corner.append(
                [jnp.take_along_axis(in_ref[d, i], pick, axis=1) for i in range(3)]
            )
        e1 = [corner[1][i] - corner[0][i] for i in range(3)]
        e2 = [corner[2][i] - corner[0][i] for i in range(3)]
        cx = e1[1] * e2[2] - e1[2] * e2[1]
        cy = e1[2] * e2[0] - e1[0] * e2[2]
        cz = e1[0] * e2[1] - e1[1] * e2[0]
        weight = jnp.sqrt(cx * cx + cy * cy + cz * cz + area_floor) / 6.0
        for s in range(3):
            for i in range(3):
                point = sum((big if m == s else small) * corner[m][i] for m in range(3))
                geo_ref[d, pl.ds((3 * s + i) * cap, cap), :] = point
        for i in range(3):
            geo_ref[d, pl.ds((9 + i) * cap, cap), :] = weight * in_ref[d, 6 + i]
        geo_ref[d, pl.ds(12 * cap, cap), :] = weight
        return 0

    lax.fori_loop(0, n, body, 0)


def to_columns(geo_ref, col_ref):
    def body(d, _):
        col_ref[d] = geo_ref[d].T
        return 0

    lax.fori_loop(0, geo_ref.shape[0], body, 0)


def spread(tile, lane):
    return jnp.take_along_axis(tile, jnp.full(tile.shape, lane, jnp.int32), axis=1)


def apply_tile(mats, ya, yb, second):
    kxx, kxy, kxz, kyy, kyz, kzz = mats
    full = ((kxx, kxy, kxz), (kxy, kyy, kyz), (kxz, kyz, kzz))
    firsts = [full[i][0] * yb[0] + full[i][1] * yb[1] + full[i][2] * yb[2] for i in range(3)]
    second = [
        second[j] + (full[0][j] * ya[0] + full[1][j] * ya[1] + full[2][j] * ya[2])
        for j in range(3)
    ]
    return [jnp.sum(t, axis=1, keepdims=True) for t in firsts], second


def keep_first(first_ref, sums, pair, t):
    block = pair // 32
    lane0 = (pair % 32) * 4
    lane = lax.broadcasted_iota(jnp.int32, (8, 128), 1)
    tile = first_ref[block, pl.ds(8 * t, 8), :]
    for i in range(3):
        tile = jnp.where(lane == lane0 + i, sums[i], tile)
    first_ref[block, pl.ds(8 * t, 8), :] = tile


def return_terms(idx_ref, first_ref, second_ref, weight_row, out_ref, *, count):
    blocks = first_ref.shape[0]
    for b in range(blocks):
        first_ref[b] = first_ref[b].T

    def body(p, _):
        oa, ra = idx_ref[0, p], idx_ref[1, p]
        ob, rb = idx_ref[0, count + p], idx_ref[1, count + p]
        wa = weight_row(oa, ra)
        wb = weight_row(ob, rb)
        for i in range(3):
            out_ref[oa, i, pl.ds(ra, 1), :] = (
                wa * first_ref[p // 32, pl.ds((p % 32) * 4 + i, 1), :]
            )
            out_ref[ob, i, pl.ds(rb, 1), :] = wb * jnp.sum(
                second_ref[p, i], axis=0, keepdims=True
            )
        return 0

    lax.fori_loop(0, count, body, 0, unroll=2)


def build_kernel(
    idx_ref, in_ref, k_ref, out_ref, w_ref, geo_ref, col_ref, first_ref, second_ref, *, cap, count
):
    step = pl.program_id(0)
    group = k_ref.shape[0]
    n = in_ref.shape[0]

    @pl.when(step == 0)
    def _():
        slot_geometry(in_ref, geo_ref, cap=cap)
        to_columns(geo_ref, col_ref)
        w_ref[...] = geo_ref[:, pl.ds(12 * cap, cap), :]

    def pair_body(g, _):
        pair = step * group + g
        oa, ra = idx_ref[0, pair], idx_ref[1, pair]
        ob, rb = idx_ref[0, count + pair], idx_ref[1, count + pair]
        row = [
            jnp.broadcast_to(geo_ref[ob, pl.ds(c * cap + rb, 1), :], (8, 128)) for c in range(12)
        ]

        def tile_body(t, second):
            cols = col_ref[oa, pl.ds(8 * t, 8), :]
            col = [spread(cols, c * cap + ra) for c in range(12)]
            su = sv = xx = xy = xz = yy = yz = None
            for s in range(3):
                for q in range(3):
                    x = col[3 * s] - row[3 * q]
                    y = col[3 * s + 1] - row[3 * q + 1]
                    z = col[3 * s + 2] - row[3 * q + 2]
                    u = lax.rsqrt(x * x + y * y + z * z + soft_sq)
                    v = u * u * u
                    vx = v * x
                    vy = v * y
                    if su is None:
                        su, sv = u, v
                        xx, xy, xz, yy, yz = vx * x, vx * y, vx * z, vy * y, vy * z
                    else:
                        su, sv = su + u, sv + v
                        xx, xy, xz = xx + vx * x, xy + vx * y, xz + vx * z
                        yy, yz = yy + vy * y, yz + vy * z
            zz = su - soft_sq * sv - xx - yy
            diag = kelvin_diag * su
            mats = (xx + diag, xy, xz, yy + diag, yz, zz + diag)
            for m in range(6):
                k_ref[g, m, pl.ds(8 * t, 8), :] = mats[m]
            sums, second = apply_tile(mats, col[9:12], row[9:12], second)
            keep_first(first_ref, sums, pair, t)
            return second

        zero = jnp.zeros((8, 128), f32)
        second = lax.fori_loop(0, 16, tile_body, [zero, zero, zero])
        for i in range(3):
            second_ref[pair, i] = second[i]
        return 0

    lax.fori_loop(0, group, pair_body, 0)

    @pl.when(step == pl.num_programs(0) - 1)
    def _():
        return_terms(
            idx_ref,
            first_ref,
            second_ref,
            lambda o, r: w_ref[o, pl.ds(r, 1), :],
            out_ref,
            count=count,
        )


def apply_kernel(
    idx_ref, x_ref, w_ref, k_ref, out_ref, geo_ref, col_ref, first_ref, second_ref, *, cap, count
):
    step = pl.program_id(0)
    group = k_ref.shape[0]
    n = x_ref.shape[0]

    @pl.when(step == 0)
    def _():

        def body(d, _):
            for i in range(3):
                geo_ref[d, pl.ds(i * cap, cap), :] = w_ref[d] * x_ref[d, i]
            return 0

        lax.fori_loop(0, n, body, 0)
        to_columns(geo_ref, col_ref)

    def pair_body(g, _):
        pair = step * group + g
        oa, ra = idx_ref[0, pair], idx_ref[1, pair]
        ob, rb = idx_ref[0, count + pair], idx_ref[1, count + pair]
        row = [
            jnp.broadcast_to(geo_ref[ob, pl.ds(c * cap + rb, 1), :], (8, 128)) for c in range(3)
        ]

        def tile_body(t, second):
            cols = col_ref[oa, pl.ds(8 * t, 8), :]
            col = [spread(cols, c * cap + ra) for c in range(3)]
            mats = [k_ref[g, m, pl.ds(8 * t, 8), :] for m in range(6)]
            sums, second = apply_tile(mats, col, row, second)
            keep_first(first_ref, sums, pair, t)
            return second

        zero = jnp.zeros((8, 128), f32)
        second = lax.fori_loop(0, 16, tile_body, [zero, zero, zero], unroll=4)
        for i in range(3):
            second_ref[pair, i] = second[i]
        return 0

    lax.fori_loop(0, group, pair_body, 0)

    @pl.when(step == pl.num_programs(0) - 1)
    def _():
        return_terms(
            idx_ref,
            first_ref,
            second_ref,
            lambda o, r: w_ref[o, pl.ds(r, 1), :],
            out_ref,
            count=count,
        )


def add_up(ask_ref, near_ref, far_ref, accs, out_ref, *, cap):
    clusters = out_ref.shape[1]
    for acc in accs:
        acc[...] = jnp.zeros(acc.shape, f32)

    def body(d, _):
        for s in range(cap):
            cn = ask_ref[d, s]
            cf = ask_ref[d, cap + s]
            for i in range(3):
                accs[i][pl.ds(cn, 1), :] += near_ref[d, i, pl.ds(s, 1), :]
                accs[3 + i][pl.ds(cf, 1), :] += far_ref[d, i, pl.ds(s, 1), :]
        return 0

    lax.fori_loop(0, near_ref.shape[0], body, 0)
    for i in range(3):
        out_ref[i] = accs[i][pl.ds(0, clusters), :] + accs[3 + i][pl.ds(0, clusters), :]


def merge_kernel(ask_ref, rn_ref, rf_ref, out_ref, near_ref, far_ref, *accs, cap):
    add_up(ask_ref, rn_ref, rf_ref, accs, out_ref, cap=cap)
    last = out_ref.shape[1] - 1

    def body(d, _):
        for s in range(cap):
            cn = jnp.minimum(ask_ref[d, s], last)
            cf = jnp.minimum(ask_ref[d, cap + s], last)
            for i in range(3):
                near_ref[d, i, pl.ds(s, 1), :] = out_ref[i, pl.ds(cn, 1), :]
                far_ref[d, i, pl.ds(s, 1), :] = out_ref[i, pl.ds(cf, 1), :]
        return 0

    lax.fori_loop(0, near_ref.shape[0], body, 0)


PRODUCTS = ((0, 0), (0, 1), (1, 1), (0, 2), (1, 2), (2, 2))


def gram_kernel(ask_ref, rn_ref, rf_ref, v0_ref, v1_ref, out_ref, part_ref, *accs, cap):
    add_up(ask_ref, rn_ref, rf_ref, accs, out_ref, cap=cap)
    clusters = out_ref.shape[1]
    refs = (v0_ref, v1_ref, out_ref)
    zero = jnp.zeros((8, 128), f32)
    totals = [(zero, zero)] * 6
    for i in range(3):

        def body(t, totals):
            tiles = [ref[i, pl.ds(8 * t, 8), :] for ref in refs]
            halves = [split(tile) for tile in tiles]
            new = []
            for k, (a, b) in enumerate(PRODUCTS):
                (ah, al), (bh, bl) = halves[a], halves[b]
                p = tiles[a] * tiles[b]
                e = ((ah * bh - p) + ah * bl + al * bh) + al * bl
                hi, lo = totals[k]
                s, err = two_sum(hi, p)
                new.append((s, lo + (err + e)))
            return new

        totals = lax.fori_loop(0, clusters // 8, body, totals)
    hi = jnp.concatenate([t[0] for t in totals], axis=0)
    lo = jnp.concatenate([t[1] for t in totals], axis=0)
    for shift in (64, 32, 16, 8, 4, 2, 1):
        hi, lo = dd_add((hi, lo), (pltpu.roll(hi, shift, 1), pltpu.roll(lo, shift, 1)))
    lane = lax.broadcasted_iota(jnp.int32, (8, 128), 1)
    shi = slo = zero
    for k in range(6):
        shi = jnp.where(lane == k, hi[8 * k : 8 * k + 8], shi)
        slo = jnp.where(lane == k, lo[8 * k : 8 * k + 8], slo)
    for shift in (4, 2, 1):
        shi, slo = dd_add((shi, slo), (pltpu.roll(shi, shift, 0), pltpu.roll(slo, shift, 0)))
    packed = jnp.where(lane < 8, shi, pltpu.roll(slo, 8, 1))
    part_ref[...] = jnp.broadcast_to(packed[0:1, :], part_ref.shape)


def final_kernel(part_ref, v0_ref, v1_ref, v2_ref, basis_ref, hess_ref, *, size_all):
    hi = part_ref[...]
    lo = pltpu.roll(hi, 120, 1)
    rows = hi.shape[0]
    while rows > 1:
        half = rows // 2
        hi, lo = dd_add((hi[:half], lo[:half]), (hi[half:], lo[half:]))
        rows = half
    inv = 1.0 / size_all
    hi, lo = dd_scale((hi, lo), jnp.full(hi.shape, inv, f32)) if size_all & (size_all - 1) == 0 else dd_div_const(hi, lo, size_all)
    g = [(hi[:, k : k + 1], lo[:, k : k + 1]) for k in range(6)]
    g00, g01, g11, g02, g12, g22 = g
    eps = jnp.full((1, 1), norm_eps, f32)
    none = jnp.zeros((1, 1), f32)
    s2 = dd_add(g00, (eps, none))
    s = jnp.sqrt(s2[0])
    p = g01[0] / s2[0]
    r1 = dd_add(g11, dd_scale(dd_add(dd_scale(g00, p), dd_scale(g01, none - 2.0)), p))
    nf = jnp.sqrt(jnp.maximum(r1[0], 0.0) / s2[0] + norm_eps)
    snf = s * nf
    c0 = dd_add(g02, dd_scale(g01, -p))
    pc = c0[0] / (s2[0] * nf)
    c1 = dd_add(dd_add(g12, dd_scale(g11, -p)), dd_scale(c0, -p))
    ps = c1[0] / (s2[0] * nf * nf)
    a1 = -(p + ps)
    a0 = ps * p - pc * nf
    t2 = dd_add(g22, dd_scale(dd_add(dd_scale(g12, a1), dd_scale(g02, a0)), none + 2.0))
    t1 = dd_scale(dd_add(dd_scale(g11, a1), dd_scale(g01, 2.0 * a0)), a1)
    t0 = dd_scale(dd_scale(g00, a0), a0)
    w2 = dd_add(dd_add(t2, t1), t0)
    n2 = jnp.sqrt(jnp.maximum(w2[0], 0.0) / (snf * snf) + norm_eps)
    k1 = 1.0 / snf
    k2 = 1.0 / (snf * n2)
    for i in range(3):
        v0, v1, v2 = v0_ref[i], v1_ref[i], v2_ref[i]
        basis_ref[0, i] = (v1 - p * v0) * k1
        basis_ref[1, i] = (v2 + a1 * v1 + a0 * v0) * k2
    top = jnp.concatenate([p, nf, none], axis=1)
    bottom = jnp.concatenate([pc, ps, n2], axis=1)
    hess_ref[...] = jnp.concatenate([top, bottom], axis=0)


def dd_div_const(hi, lo, size_all):
    d = jnp.full(hi.shape, float(size_all), f32)
    q = hi / d
    p, e = two_prod(q, d)
    rest = ((hi - p) - e) + lo
    return q, rest / d


def per_device(
    right_side, vertices, panels, near_owner, near_local, far_owner, far_local, far_left, far_right
):
    n = lax.axis_size("dev")
    clusters, _, width = right_side.shape
    near_count = near_owner.shape[0]
    far_count = far_owner.shape[0]
    cap = max(2, 4 * near_count // n)
    size_all = clusters * n * 3 * width
    x0 = right_side.transpose(1, 0, 2)
    shape = jax.ShapeDtypeStruct

    def exchange(block):
        return lax.all_to_all(block, "dev", split_axis=0, concat_axis=0, tiled=True)

    slots = max(128, 2 * cap)
    ask, idx = pl.pallas_call(
        lambda *refs: prep_kernel(*refs, cap=cap, trash=clusters),
        out_shape=(shape((n, slots), jnp.int32), shape((8, 2 * near_count), jnp.int32)),
        compiler_params=params(),
        name="prep",
    )(near_owner.T, near_local.T, far_owner.T, far_local.T)
    asked = exchange(ask)

    near_out, far_out = pl.pallas_call(
        lambda *refs: pack_kernel(*refs, cap=cap),
        out_shape=(shape((n, 9, cap, width), f32), shape((n, 3, cap, width), f32)),
        in_specs=[SM, VM, VM, VM],
        scratch_shapes=[pltpu.VMEM((3, clusters, width), f32)],
        compiler_params=params(),
        name="pack",
    )(asked, x0, vertices.transpose(1, 0, 2), panels.transpose(1, 0, 2))

    def far_product(received):
        return pl.pallas_call(
            far_kernel,
            out_shape=shape((n, 3, cap, width), f32),
            in_specs=[SM, VM, VM, VM],
            compiler_params=params(),
            name="far",
        )(idx, received, far_left, far_right)

    far_in = exchange(far_out)
    near_in = exchange(near_out)
    far_back = exchange(far_product(far_in))

    group = 4
    steps = near_count // group
    blocks = -(-near_count // 32)
    rows = -(-13 * cap // 128) * 128
    k_spec = pl.BlockSpec((group, 6, width, width), lambda g: (g, 0, 0, 0))

    def whole(*dims):
        return pl.BlockSpec(dims, lambda g: (0,) * len(dims))

    scratch = [
        pltpu.VMEM((n, rows, width), f32),
        pltpu.VMEM((n, width, rows), f32),
        pltpu.VMEM((blocks, width, 128), f32),
        pltpu.VMEM((near_count, 3, 8, width), f32),
    ]
    stored, near_terms, weights = pl.pallas_call(
        lambda *refs: build_kernel(*refs, cap=cap, count=near_count),
        out_shape=(
            shape((near_count, 6, width, width), f32),
            shape((n, 3, cap, width), f32),
            shape((n, cap, width), f32),
        ),
        grid=(steps,),
        in_specs=[SM, whole(n, 9, cap, width)],
        out_specs=(k_spec, whole(n, 3, cap, width), whole(n, cap, width)),
        scratch_shapes=scratch,
        compiler_params=params(),
        name="build",
    )(idx, near_in)
    near_back = exchange(near_terms)

    accs = [pltpu.VMEM((clusters + 8, width), f32)] * 6
    x1, near_out2, far_out2 = pl.pallas_call(
        lambda *refs: merge_kernel(*refs, cap=cap),
        out_shape=(
            shape((3, clusters, width), f32),
            shape((n, 3, cap, width), f32),
            shape((n, 3, cap, width), f32),
        ),
        in_specs=[SM, VM, VM],
        scratch_shapes=accs,
        compiler_params=params(),
        name="merge",
    )(asked, near_back, far_back)
    far_in2 = exchange(far_out2)
    near_in2 = exchange(near_out2)
    far_back2 = exchange(far_product(far_in2))
    rows2 = 128
    scratch2 = [
        pltpu.VMEM((n, rows2, width), f32),
        pltpu.VMEM((n, width, rows2), f32),
        pltpu.VMEM((blocks, width, 128), f32),
        pltpu.VMEM((near_count, 3, 8, width), f32),
    ]
    near_terms2 = pl.pallas_call(
        lambda *refs: apply_kernel(*refs, cap=cap, count=near_count),
        out_shape=shape((n, 3, cap, width), f32),
        grid=(steps,),
        in_specs=[SM, whole(n, 3, cap, width), whole(n, cap, width), k_spec],
        out_specs=whole(n, 3, cap, width),
        scratch_shapes=scratch2,
        compiler_params=params(),
        name="apply",
    )(idx, near_in2, weights, stored)
    near_back2 = exchange(near_terms2)

    x2, part = pl.pallas_call(
        lambda *refs: gram_kernel(*refs, cap=cap),
        out_shape=(shape((3, clusters, width), f32), shape((n, 128), f32)),
        in_specs=[SM, VM, VM, VM, VM],
        scratch_shapes=accs,
        compiler_params=params(),
        name="gram",
    )(asked, near_back2, far_back2, x0, x1)
    parts = exchange(part)
    basis, hess = pl.pallas_call(
        lambda *refs: final_kernel(*refs, size_all=size_all),
        out_shape=(shape((2, 3, clusters, width), f32), shape((2, 3), f32)),
        compiler_params=params(),
        name="final",
    )(parts, x0, x1, x2)
    return (basis.transpose(0, 2, 1, 3), hess.T)


def solution(mesh):
    per_cluster = P("dev", None, None)
    per_pair = P("dev", None)
    in_specs = (per_cluster,) * 3 + (per_pair,) * 4 + (per_cluster,) * 2
    out_specs = (P(None, "dev", None, None), P())
    return jax.shard_map(
        per_device, mesh=mesh, in_specs=in_specs, out_specs=out_specs, check_vma=False
    )
```

```python
import jax
import jax.numpy as jnp
from jax import lax
from jax.experimental import pallas as pl
from jax.experimental.pallas import tpu as pltpu
from jax.sharding import PartitionSpec as P


soft_sq = 0.0025
area_floor = 6.25e-06
kelvin_diag = 1.8
norm_eps = 1e-06
big = 2.0 / 3.0
small = 1.0 / 6.0
BUILD_UNROLL = 4
APPLY_UNROLL = 16
f32 = jnp.float32
VM = pl.BlockSpec(memory_space=pltpu.VMEM)
SM = pl.BlockSpec(memory_space=pltpu.SMEM)
ANY = pl.BlockSpec(memory_space=pl.ANY)


def params(**kw):
    return pltpu.CompilerParams(vmem_limit_bytes=60 << 20, **kw)


def cost(us):
    return pl.CostEstimate(flops=0, transcendentals=0, bytes_accessed=int(us * 3.0e6))


def two_sum(a, b):
    s = a + b
    t = s - a
    return s, (a - (s - t)) + (b - t)


def split(a):
    c = a * 4097.0
    hi = c - (c - a)
    return hi, a - hi


def two_prod(a, b):
    p = a * b
    ah, al = split(a)
    bh, bl = split(b)
    return p, ((ah * bh - p) + ah * bl + al * bh) + al * bl


def dd_add(x, y):
    s, e = two_sum(x[0], y[0])
    e = e + (x[1] + y[1])
    hi = s + e
    return hi, e - (hi - s)


def dd_scale(x, f):
    p, e = two_prod(x[0], f)
    e = e + x[1] * f
    hi = p + e
    return hi, e - (hi - p)


def prep_kernel(no_ref, nl_ref, fo_ref, fl_ref, ask_ref, idx_ref, *, cap, trash):
    n = ask_ref.shape[0]
    width = 2 * no_ref.shape[1]
    ask = jnp.full(ask_ref.shape, float(trash), f32)
    rows = []
    for part, (o_ref, l_ref) in enumerate(((no_ref, nl_ref), (fo_ref, fl_ref))):
        owner = jnp.concatenate([o_ref[0:1, :], o_ref[1:2, :]], axis=1).astype(f32)
        local = jnp.concatenate([l_ref[0:1, :], l_ref[1:2, :]], axis=1).astype(f32)
        across = jnp.broadcast_to(owner, (width, width))
        down = across.T
        row = lax.broadcasted_iota(jnp.int32, (width, width), 0)
        col = lax.broadcasted_iota(jnp.int32, (width, width), 1)
        earlier = jnp.where((across == down) & (row < col), 1.0, 0.0)
        rank = jnp.sum(earlier, axis=0, keepdims=True)
        dest = lax.broadcasted_iota(jnp.int32, (n, width), 0).astype(f32)
        lhs = jnp.where(dest == owner, local + 1.0, 0.0).astype(jnp.bfloat16)
        slot = lax.broadcasted_iota(jnp.int32, (ask_ref.shape[1], width), 0).astype(f32)
        rhs = jnp.where(slot == rank + float(part * cap), 1.0, 0.0).astype(jnp.bfloat16)
        found = lax.dot_general(
            lhs, rhs, (((1,), (1,)), ((), ())), preferred_element_type=f32
        )
        ask = jnp.where(found > 0.5, found - 1.0, ask)
        rows += [owner, rank]
    ask_ref[...] = ask.astype(jnp.int32)
    idx_ref[...] = jnp.concatenate(rows + rows, axis=0).astype(jnp.int32)


def pack_rows(ask_ref, sources, out_ref):
    last = sources[0].shape[1] - 1

    def body(d, _):
        for s in range(out_ref.shape[2]):
            c = jnp.minimum(ask_ref[d, s], last)
            for k, source in enumerate(sources):
                for i in range(3):
                    out_ref[d, 3 * k + i, pl.ds(s, 1), :] = source[i, pl.ds(c, 1), :]
        return 0

    lax.fori_loop(0, out_ref.shape[0], body, 0, unroll=2)


def pack_kernel(ask_ref, x_ref, out_ref):
    pack_rows(ask_ref, (x_ref,), out_ref)


def pack_near_kernel(ask_ref, v_ref, p_ref, out_ref, pan_ref):
    pan_ref[...] = p_ref[...].astype(f32)
    pack_rows(ask_ref, (v_ref, pan_ref), out_ref)


def far_kernel(idx_ref, x_ref, l_ref, r_ref, out_ref, *, cap):
    count = l_ref.shape[0]

    def body(f, _):
        oa, ra = idx_ref[2, f], idx_ref[3, f]
        ob, rb = idx_ref[2, count + f], idx_ref[3, count + f]
        left = [l_ref[f, :, pl.ds(128 * i, 128)] for i in range(3)]
        right = [r_ref[f, :, pl.ds(128 * i, 128)] for i in range(3)]
        xa = [x_ref[oa, i, pl.ds(cap + ra, 1), :] for i in range(3)]
        xb = [x_ref[ob, i, pl.ds(cap + rb, 1), :] for i in range(3)]
        coef_b = jnp.sum(sum(right[i] * xb[i] for i in range(3)), axis=1, keepdims=True)
        coef_a = jnp.sum(sum(left[i] * xa[i] for i in range(3)), axis=1, keepdims=True)
        for i in range(3):
            out_ref[oa, i, pl.ds(ra, 1), :] = jnp.sum(left[i] * coef_b, axis=0, keepdims=True)
            out_ref[ob, i, pl.ds(rb, 1), :] = jnp.sum(right[i] * coef_a, axis=0, keepdims=True)
        return 0

    lax.fori_loop(0, count, body, 0, unroll=4)


def slot_geometry(in_ref, geo_ref, *, cap):
    n = in_ref.shape[0]

    def body(d, _):
        corner = []
        for m in range(3):
            pick = in_ref[d, 3 + m].astype(jnp.int32)
            corner.append(
                [jnp.take_along_axis(in_ref[d, i], pick, axis=1) for i in range(3)]
            )
        e1 = [corner[1][i] - corner[0][i] for i in range(3)]
        e2 = [corner[2][i] - corner[0][i] for i in range(3)]
        cx = e1[1] * e2[2] - e1[2] * e2[1]
        cy = e1[2] * e2[0] - e1[0] * e2[2]
        cz = e1[0] * e2[1] - e1[1] * e2[0]
        weight = jnp.sqrt(cx * cx + cy * cy + cz * cz + area_floor) / 6.0
        for s in range(3):
            for i in range(3):
                point = sum((big if m == s else small) * corner[m][i] for m in range(3))
                geo_ref[d, pl.ds((3 * s + i) * cap, cap), :] = point
        geo_ref[d, pl.ds(9 * cap, cap), :] = weight
        return 0

    lax.fori_loop(0, n, body, 0)


def pair_ends(idx_ref, pair, count):
    return (
        (idx_ref[0, pair], idx_ref[1, pair]),
        (idx_ref[0, count + pair], idx_ref[1, count + pair]),
    )


def skew_start(idx_ref, parts, base_ref, pair, *, cap, count):
    (oa, ra), _ = pair_ends(idx_ref, pair, count)
    at = 0
    for ref, comps in parts:
        for c in range(comps):
            row = jnp.broadcast_to(ref[oa, pl.ds(c * cap + ra, 1), :], (8, 128))
            base_ref[at + c] = pltpu.roll(row, 0, 1, stride=1, stride_axis=0)
        at += comps


def skew_tile(base_ref, dst_ref, t):
    for c in range(base_ref.shape[0]):
        dst_ref[c, pl.ds(pl.multiple_of(8 * t, 8), 8), :] = pltpu.roll(base_ref[c], 8 * t, 1)


def weighted(geo_ref, x_ref, y_ref, *, cap):
    def body(d, _):
        weight = geo_ref[d, pl.ds(9 * cap, cap), :]
        for i in range(3):
            y_ref[d, pl.ds(i * cap, cap), :] = weight * x_ref[d, i, pl.ds(0, cap), :]
        return 0

    lax.fori_loop(0, x_ref.shape[0], body, 0, unroll=4)


def apply_tile(mats, ya, yb, second):
    kxx, kxy, kxz, kyy, kyz, kzz = mats
    full = ((kxx, kxy, kxz), (kxy, kyy, kyz), (kxz, kyz, kzz))
    firsts = [full[i][0] * yb[0] + full[i][1] * yb[1] + full[i][2] * yb[2] for i in range(3)]
    second = [
        second[j] + (full[0][j] * ya[0] + full[1][j] * ya[1] + full[2][j] * ya[2])
        for j in range(3)
    ]
    return firsts, second


def return_terms(idx_ref, geo_ref, first_ref, second_ref, out_ref, *, cap, count):
    def body(p, _):
        (oa, ra), (ob, rb) = pair_ends(idx_ref, p, count)
        wa = geo_ref[oa, pl.ds(9 * cap + ra, 1), :]
        wb = geo_ref[ob, pl.ds(9 * cap + rb, 1), :]
        for i in range(3):
            first = first_ref[p, i]
            for half in (4, 2, 1):
                first = first + pltpu.roll(pltpu.roll(first, 8 - half, 0), 128 - half, 1)
            out_ref[oa, i, pl.ds(ra, 1), :] = wa * first[0:1]
            second = jnp.sum(second_ref[p, i], axis=0, keepdims=True)
            out_ref[ob, i, pl.ds(rb, 1), :] = wb * second
        return 0

    lax.fori_loop(0, count, body, 0, unroll=4)


def near_tile(col, row):
    su = sv = xx = xy = xz = yy = yz = None
    for s in range(3):
        for q in range(3):
            x = col[3 * s] - row[3 * q]
            y = col[3 * s + 1] - row[3 * q + 1]
            z = col[3 * s + 2] - row[3 * q + 2]
            u = lax.rsqrt(x * x + y * y + z * z + soft_sq)
            v = u * u * u
            vx = v * x
            vy = v * y
            if su is None:
                su, sv = u, v
                xx, xy, xz, yy, yz = vx * x, vx * y, vx * z, vy * y, vy * z
            else:
                su, sv = su + u, sv + v
                xx, xy, xz = xx + vx * x, xy + vx * y, xz + vx * z
                yy, yz = yy + vy * y, yz + vy * z
    zz = su - soft_sq * sv - xx - yy
    diag = kelvin_diag * su
    return (xx + diag, xy, xz, yy + diag, yz, zz + diag)


def sweep_pairs(
    idx_ref, parts, bases, bufs, tile_mats, sums, *, step, pair0, pairs, group, cap, count, unroll
):
    def two_pairs(h, _):
        for j in range(2):
            src, dst, base = bufs[j], bufs[1 - j], bases[j]
            g = 2 * h + j
            local = step * group + g
            pair = pair0 + local
            following = jnp.minimum(pair + 1, pair0 + pairs - 1)
            skew_start(idx_ref, parts, base, following, cap=cap, count=count)
            _, (ob, rb) = pair_ends(idx_ref, pair, count)
            row = [
                jnp.broadcast_to(ref[ob, pl.ds(c * cap + rb, 1), :], (8, 128))
                for ref, comps in parts
                for c in range(comps)
            ]
            comps = len(row)

            def tile_body(t, carry, g=g, src=src, dst=dst, base=base, row=row):
                if sums is not None:
                    held, first, second = carry
                    back = (128 - 8 * (t - 1)) % 128
                    first = [first[i] + pltpu.roll(held[i], back, 1) for i in range(3)]
                skew_tile(base, dst, t)
                tile = pl.ds(pl.multiple_of(8 * t, 8), 8)
                col = [src[c, tile, :] for c in range(comps)]
                mats = tile_mats(g, tile, col, row)
                if sums is None:
                    return carry
                held, second = apply_tile(mats, col[comps - 3 :], row[comps - 3 :], second)
                return held, first, second

            zero = [jnp.zeros((8, 128), f32)] * 3
            start = 0 if sums is None else (zero, zero, zero)
            carry = lax.fori_loop(0, 16, tile_body, start, unroll=unroll)
            if sums is not None:
                held, first, second = carry
                for i in range(3):
                    sums[0][local, i] = first[i] + pltpu.roll(held[i], 8, 1)
                    sums[1][local, i] = second[i]
        return 0

    lax.fori_loop(0, group // 2, two_pairs, 0)


def skew_first_pair(idx_ref, parts, base, buf, pair, *, cap, count):
    skew_start(idx_ref, parts, base, pair, cap=cap, count=count)

    def body(t, _):
        skew_tile(base, buf, t)
        return 0

    lax.fori_loop(0, 16, body, 0, unroll=4)


def build_blocks(idx_ref, geo_ref, k_ref, base0, base1, buf0, buf1, *, pair0, pairs, cap, count):
    step = pl.program_id(0)
    parts = ((geo_ref, 9),)

    @pl.when(step == 0)
    def _():
        skew_first_pair(idx_ref, parts, base1, buf0, pair0, cap=cap, count=count)

    def tile_mats(g, tile, col, row):
        mats = near_tile(col, row)
        for m in range(6):
            k_ref[g, m, tile, :] = mats[m]
        return mats

    sweep_pairs(
        idx_ref, parts, (base0, base1), (buf0, buf1), tile_mats, None,
        step=step, pair0=pair0, pairs=pairs, group=k_ref.shape[0], cap=cap, count=count,
        unroll=BUILD_UNROLL,
    )


def build_kernel(idx_ref, in_ref, k_ref, geo_ref, *skews, pairs, cap, count):
    @pl.when(pl.program_id(0) == 0)
    def _():
        slot_geometry(in_ref, geo_ref, cap=cap)

    build_blocks(idx_ref, geo_ref, k_ref, *skews, pair0=0, pairs=pairs, cap=cap, count=count)


def build_rest_kernel(idx_ref, geo_ref, old_ref, far_ref, k_ref, *skews, pair0, cap, count):
    build_blocks(
        idx_ref, geo_ref, k_ref, *skews, pair0=pair0, pairs=count - pair0, cap=cap, count=count
    )


def apply_kernel(
    idx_ref, geo_ref, x_ref, k_ref, out_ref,
    first_ref, second_ref, y_ref, base0, base1, buf0, buf1, *, cap, count,
):
    step = pl.program_id(0)
    parts = ((y_ref, 3),)

    @pl.when(step == 0)
    def _():
        weighted(geo_ref, x_ref, y_ref, cap=cap)
        skew_first_pair(idx_ref, parts, base1, buf0, 0, cap=cap, count=count)

    def tile_mats(g, tile, col, row):
        return [k_ref[g, m, tile, :] for m in range(6)]

    sweep_pairs(
        idx_ref, parts, (base0, base1), (buf0, buf1), tile_mats, (first_ref, second_ref),
        step=step, pair0=0, pairs=count, group=k_ref.shape[0], cap=cap, count=count,
        unroll=APPLY_UNROLL,
    )

    @pl.when(step == pl.num_programs(0) - 1)
    def _():
        return_terms(idx_ref, geo_ref, first_ref, second_ref, out_ref, cap=cap, count=count)


def add_up(ask_ref, near_ref, far_ref, accs, out_ref, *, cap):
    clusters = out_ref.shape[1]
    for acc in accs:
        acc[...] = jnp.zeros(acc.shape, f32)

    def body(d, _):
        for s in range(cap):
            cn = ask_ref[d, s]
            cf = ask_ref[d, cap + s]
            for i in range(3):
                accs[i][pl.ds(cn, 1), :] += near_ref[d, i, pl.ds(s, 1), :]
                accs[3 + i][pl.ds(cf, 1), :] += far_ref[d, i, pl.ds(s, 1), :]
        return 0

    lax.fori_loop(0, near_ref.shape[0], body, 0)
    for i in range(3):
        out_ref[i] = accs[i][pl.ds(0, clusters), :] + accs[3 + i][pl.ds(0, clusters), :]


def merge_kernel(ask_ref, rn_ref, rf_ref, out_ref, pack_ref, *accs, cap):
    add_up(ask_ref, rn_ref, rf_ref, accs, out_ref, cap=cap)
    pack_rows(ask_ref, (out_ref,), pack_ref)


PRODUCTS = ((0, 0), (0, 1), (1, 1), (0, 2), (1, 2), (2, 2))


def gram_kernel(ask_ref, rn_ref, rf_ref, v0_ref, v1_ref, out_ref, part_ref, *accs, cap):
    add_up(ask_ref, rn_ref, rf_ref, accs, out_ref, cap=cap)
    clusters = out_ref.shape[1]
    refs = (v0_ref, v1_ref, out_ref)
    zero = jnp.zeros((8, 128), f32)
    totals = [(zero, zero)] * 6
    for i in range(3):

        def body(t, totals):
            tiles = [ref[i, pl.ds(8 * t, 8), :] for ref in refs]
            halves = [split(tile) for tile in tiles]
            new = []
            for k, (a, b) in enumerate(PRODUCTS):
                (ah, al), (bh, bl) = halves[a], halves[b]
                p = tiles[a] * tiles[b]
                e = ((ah * bh - p) + ah * bl + al * bh) + al * bl
                hi, lo = totals[k]
                s, err = two_sum(hi, p)
                new.append((s, lo + (err + e)))
            return new

        totals = lax.fori_loop(0, clusters // 8, body, totals)
    hi = jnp.concatenate([t[0] for t in totals], axis=0)
    lo = jnp.concatenate([t[1] for t in totals], axis=0)
    for shift in (64, 32, 16, 8, 4, 2, 1):
        hi, lo = dd_add((hi, lo), (pltpu.roll(hi, shift, 1), pltpu.roll(lo, shift, 1)))
    lane = lax.broadcasted_iota(jnp.int32, (8, 128), 1)
    shi = slo = zero
    for k in range(6):
        shi = jnp.where(lane == k, hi[8 * k : 8 * k + 8], shi)
        slo = jnp.where(lane == k, lo[8 * k : 8 * k + 8], slo)
    for shift in (4, 2, 1):
        shi, slo = dd_add((shi, slo), (pltpu.roll(shi, shift, 0), pltpu.roll(slo, shift, 0)))
    packed = jnp.where(lane < 8, shi, pltpu.roll(slo, 8, 1))
    part_ref[...] = jnp.broadcast_to(packed[0:1, :], part_ref.shape)


def final_kernel(part_ref, v0_ref, v1_ref, v2_ref, basis_ref, hess_ref, *, size_all):
    hi = part_ref[...]
    lo = pltpu.roll(hi, 120, 1)
    rows = hi.shape[0]
    while rows > 1:
        half = rows // 2
        hi, lo = dd_add((hi[:half], lo[:half]), (hi[half:], lo[half:]))
        rows = half
    inv = 1.0 / size_all
    hi, lo = dd_scale((hi, lo), jnp.full(hi.shape, inv, f32)) if size_all & (size_all - 1) == 0 else dd_div_const(hi, lo, size_all)
    g = [(hi[:, k : k + 1], lo[:, k : k + 1]) for k in range(6)]
    g00, g01, g11, g02, g12, g22 = g
    eps = jnp.full((1, 1), norm_eps, f32)
    none = jnp.zeros((1, 1), f32)
    s2 = dd_add(g00, (eps, none))
    s = jnp.sqrt(s2[0])
    p = g01[0] / s2[0]
    r1 = dd_add(g11, dd_scale(dd_add(dd_scale(g00, p), dd_scale(g01, none - 2.0)), p))
    nf = jnp.sqrt(jnp.maximum(r1[0], 0.0) / s2[0] + norm_eps)
    snf = s * nf
    c0 = dd_add(g02, dd_scale(g01, -p))
    pc = c0[0] / (s2[0] * nf)
    c1 = dd_add(dd_add(g12, dd_scale(g11, -p)), dd_scale(c0, -p))
    ps = c1[0] / (s2[0] * nf * nf)
    a1 = -(p + ps)
    a0 = ps * p - pc * nf
    t2 = dd_add(g22, dd_scale(dd_add(dd_scale(g12, a1), dd_scale(g02, a0)), none + 2.0))
    t1 = dd_scale(dd_add(dd_scale(g11, a1), dd_scale(g01, 2.0 * a0)), a1)
    t0 = dd_scale(dd_scale(g00, a0), a0)
    w2 = dd_add(dd_add(t2, t1), t0)
    n2 = jnp.sqrt(jnp.maximum(w2[0], 0.0) / (snf * snf) + norm_eps)
    k1 = 1.0 / snf
    k2 = 1.0 / (snf * n2)
    for i in range(3):
        v0, v1, v2 = v0_ref[i], v1_ref[i], v2_ref[i]
        basis_ref[0, i] = (v1 - p * v0) * k1
        basis_ref[1, i] = (v2 + a1 * v1 + a0 * v0) * k2
    top = jnp.concatenate([p, nf, none], axis=1)
    bottom = jnp.concatenate([pc, ps, n2], axis=1)
    hess_ref[...] = jnp.concatenate([top, bottom], axis=0)


def dd_div_const(hi, lo, size_all):
    d = jnp.full(hi.shape, float(size_all), f32)
    q = hi / d
    p, e = two_prod(q, d)
    rest = ((hi - p) - e) + lo
    return q, rest / d


def per_device(
    right_side, vertices, panels, near_owner, near_local, far_owner, far_local, far_left, far_right
):
    n = lax.axis_size("dev")
    clusters, _, width = right_side.shape
    near_count = near_owner.shape[0]
    cap = max(2, 4 * near_count // n)
    size_all = clusters * n * 3 * width
    x0 = right_side.transpose(1, 0, 2)
    shape = jax.ShapeDtypeStruct

    def exchange(block):
        return lax.all_to_all(block, "dev", split_axis=0, concat_axis=0, tiled=True)

    slots = max(128, 2 * cap)
    ask, idx = pl.pallas_call(
        lambda *refs: prep_kernel(*refs, cap=cap, trash=clusters),
        out_shape=(shape((n, slots), jnp.int32), shape((8, 2 * near_count), jnp.int32)),
        compiler_params=params(),
        name="prep",
    )(near_owner.T, near_local.T, far_owner.T, far_local.T)
    asked = exchange(ask)

    rows3 = shape((n, 3, cap, width), f32)
    both = shape((n, 3, 2 * cap, width), f32)

    near_in = exchange(
        pl.pallas_call(
            pack_near_kernel,
            out_shape=shape((n, 6, cap, width), f32),
            in_specs=[SM, VM, VM],
            scratch_shapes=[pltpu.VMEM((3, clusters, width), f32)],
            compiler_params=params(),
            cost_estimate=cost(4.0),
            name="pack_near",
        )(asked, vertices.transpose(1, 0, 2), panels.transpose(1, 0, 2))
    )
    x0_out = pl.pallas_call(
        pack_kernel,
        out_shape=both,
        in_specs=[SM, VM],
        compiler_params=params(),
        cost_estimate=cost(3.0),
        name="pack",
    )(asked, x0)
    x0_in = exchange(x0_out)

    group = 8
    early = near_count // 2
    k_block = (group, 6, width, width)
    k_shape = shape((near_count, 6, width, width), f32)
    rows10 = (n, 10 * cap, width)

    def whole(*dims):
        return pl.BlockSpec(dims, lambda g: (0,) * len(dims))

    def skews(comps):
        return [pltpu.VMEM((comps, 8, width), f32)] * 2 + [
            pltpu.VMEM((comps, width, width), f32)
        ] * 2

    stored, geometry = pl.pallas_call(
        lambda *refs: build_kernel(*refs, pairs=early, cap=cap, count=near_count),
        out_shape=(k_shape, shape(rows10, f32)),
        grid=(early // group,),
        in_specs=[SM, whole(n, 6, cap, width)],
        out_specs=(pl.BlockSpec(k_block, lambda g: (g, 0, 0, 0)), whole(*rows10)),
        scratch_shapes=skews(9),
        compiler_params=params(),
        cost_estimate=cost(30.0),
        name="build",
    )(idx, near_in)

    def far_product(received):
        return pl.pallas_call(
            lambda *refs: far_kernel(*refs, cap=cap),
            out_shape=rows3,
            in_specs=[SM, VM, VM, VM],
            compiler_params=params(),
            cost_estimate=cost(5.0),
            name="far",
        )(idx, received, far_left, far_right)

    far_terms = far_product(x0_in)
    far_back = exchange(far_terms)
    stored = pl.pallas_call(
        lambda *refs: build_rest_kernel(*refs, pair0=early, cap=cap, count=near_count),
        out_shape=k_shape,
        grid=((near_count - early) // group,),
        in_specs=[SM, whole(*rows10), ANY, ANY],
        out_specs=pl.BlockSpec(k_block, lambda g: (g + early // group, 0, 0, 0)),
        scratch_shapes=skews(9),
        input_output_aliases={2: 0},
        compiler_params=params(),
        cost_estimate=cost(30.0),
        name="build_rest",
    )(idx, geometry, stored, far_terms)

    def apply_stored(received):
        return exchange(
            pl.pallas_call(
                lambda *refs: apply_kernel(*refs, cap=cap, count=near_count),
                out_shape=rows3,
                grid=(near_count // group,),
                in_specs=[
                    SM,
                    whole(*rows10),
                    whole(*both.shape),
                    pl.BlockSpec(k_block, lambda g: (g, 0, 0, 0)),
                ],
                out_specs=whole(n, 3, cap, width),
                scratch_shapes=[pltpu.VMEM((near_count, 3, 8, width), f32)] * 2
                + [pltpu.VMEM((n, 3 * cap, width), f32)]
                + skews(3),
                compiler_params=params(),
                cost_estimate=cost(18.0),
                name="apply",
            )(idx, geometry, received, stored)
        )

    near_back = apply_stored(x0_in)

    accs = [pltpu.VMEM((clusters + 8, width), f32)] * 6
    x1, x1_out = pl.pallas_call(
        lambda *refs: merge_kernel(*refs, cap=cap),
        out_shape=(shape((3, clusters, width), f32), both),
        in_specs=[SM, VM, VM],
        scratch_shapes=accs,
        compiler_params=params(),
        cost_estimate=cost(5.0),
        name="merge",
    )(asked, near_back, far_back)
    x1_in = exchange(x1_out)
    far_back2 = exchange(far_product(x1_in))
    near_back2 = apply_stored(x1_in)

    x2, part = pl.pallas_call(
        lambda *refs: gram_kernel(*refs, cap=cap),
        out_shape=(shape((3, clusters, width), f32), shape((n, 128), f32)),
        in_specs=[SM, VM, VM, VM, VM],
        scratch_shapes=accs,
        compiler_params=params(),
        cost_estimate=cost(5.0),
        name="gram",
    )(asked, near_back2, far_back2, x0, x1)
    parts = exchange(part)
    basis, hess = pl.pallas_call(
        lambda *refs: final_kernel(*refs, size_all=size_all),
        out_shape=(shape((2, 3, clusters, width), f32), shape((2, 3), f32)),
        compiler_params=params(),
        name="final",
    )(parts, x0, x1, x2)
    return (basis.transpose(0, 2, 1, 3), hess.T)


def solution(mesh):
    per_cluster = P("dev", None, None)
    per_pair = P("dev", None)
    in_specs = (per_cluster,) * 3 + (per_pair,) * 4 + (per_cluster,) * 2
    out_specs = (P(None, "dev", None, None), P())

    return jax.shard_map(
        per_device, mesh=mesh, in_specs=in_specs, out_specs=out_specs, check_vma=False
    )
```

```python
import jax
import jax.numpy as jnp
from jax import lax
from jax.experimental import pallas as pl
from jax.experimental.pallas import tpu as pltpu
from jax.sharding import PartitionSpec as P


soft_sq = 0.0025
area_floor = 6.25e-06
kelvin_diag = 1.8
norm_eps = 1e-06
big = 2.0 / 3.0
small = 1.0 / 6.0
BUILD_UNROLL = 4
APPLY_UNROLL = 16
f32 = jnp.float32
VM = pl.BlockSpec(memory_space=pltpu.VMEM)
SM = pl.BlockSpec(memory_space=pltpu.SMEM)
ANY = pl.BlockSpec(memory_space=pl.ANY)


def params(mib=8):
    return pltpu.CompilerParams(vmem_limit_bytes=mib << 20)


def cost(us):
    return pl.CostEstimate(flops=0, transcendentals=0, bytes_accessed=int(us * 3.0e6))


def two_sum(a, b):
    s = a + b
    t = s - a
    return s, (a - (s - t)) + (b - t)


def split(a):
    c = a * 4097.0
    hi = c - (c - a)
    return hi, a - hi


def two_prod(a, b):
    p = a * b
    ah, al = split(a)
    bh, bl = split(b)
    return p, ((ah * bh - p) + ah * bl + al * bh) + al * bl


def dd_add(x, y):
    s, e = two_sum(x[0], y[0])
    e = e + (x[1] + y[1])
    hi = s + e
    return hi, e - (hi - s)


def dd_scale(x, f):
    p, e = two_prod(x[0], f)
    e = e + x[1] * f
    hi = p + e
    return hi, e - (hi - p)


def prep_kernel(no_ref, nl_ref, fo_ref, fl_ref, ask_ref, idx_ref, *, cap, trash):
    n = ask_ref.shape[0]
    width = 2 * no_ref.shape[1]
    ask = jnp.full(ask_ref.shape, float(trash), f32)
    rows = []
    for part, (o_ref, l_ref) in enumerate(((no_ref, nl_ref), (fo_ref, fl_ref))):
        owner = jnp.concatenate([o_ref[0:1, :], o_ref[1:2, :]], axis=1).astype(f32)
        local = jnp.concatenate([l_ref[0:1, :], l_ref[1:2, :]], axis=1).astype(f32)
        across = jnp.broadcast_to(owner, (width, width))
        down = across.T
        row = lax.broadcasted_iota(jnp.int32, (width, width), 0)
        col = lax.broadcasted_iota(jnp.int32, (width, width), 1)
        earlier = jnp.where((across == down) & (row < col), 1.0, 0.0)
        rank = jnp.sum(earlier, axis=0, keepdims=True)
        dest = lax.broadcasted_iota(jnp.int32, (n, width), 0).astype(f32)
        lhs = jnp.where(dest == owner, local + 1.0, 0.0).astype(jnp.bfloat16)
        slot = lax.broadcasted_iota(jnp.int32, (ask_ref.shape[1], width), 0).astype(f32)
        rhs = jnp.where(slot == rank + float(part * cap), 1.0, 0.0).astype(jnp.bfloat16)
        found = lax.dot_general(
            lhs, rhs, (((1,), (1,)), ((), ())), preferred_element_type=f32
        )
        ask = jnp.where(found > 0.5, found - 1.0, ask)
        rows += [owner, rank]
    ask_ref[...] = ask.astype(jnp.int32)
    idx_ref[...] = jnp.concatenate(rows + rows, axis=0).astype(jnp.int32)


def pack_rows(ask_ref, fetch, out_ref, *, n, slots, kinds):
    def body(d, _):
        for s in range(slots):
            rows = fetch(ask_ref[d, s])
            for k in range(kinds):
                at = (d * kinds + k) * 3 * slots + s
                out_ref[pl.ds(at, 3, stride=slots), :] = rows[k]
        return 0

    lax.fori_loop(0, n, body, 0, unroll=2)


def cluster_rows(refs):
    clusters = refs[0].shape[0] // 3

    def fetch(c):
        c = jnp.minimum(c, clusters - 1)
        return [ref[pl.ds(c, 3, stride=clusters), :] for ref in refs]

    return fetch


def pack_kernel(ask_ref, x_ref, out_ref, *, n, slots):
    pack_rows(ask_ref, cluster_rows((x_ref,)), out_ref, n=n, slots=slots, kinds=1)


def pack_near_kernel(ask_ref, v_ref, p_ref, out_ref, pan_ref, *, n, slots):
    pan_ref[...] = p_ref[...].astype(f32)
    pack_rows(ask_ref, cluster_rows((v_ref, pan_ref)), out_ref, n=n, slots=slots, kinds=2)


def far_kernel(idx_ref, x_ref, l_ref, r_ref, out_ref, sum_ref, row_ref, *, cap):
    count = l_ref.shape[0]

    def ends(f):
        oa, ra = idx_ref[2, f], idx_ref[3, f]
        ob, rb = idx_ref[2, count + f], idx_ref[3, count + f]
        return (oa, ra), (ob, rb)

    def body(f, _):
        (oa, ra), (ob, rb) = ends(f)
        left = [l_ref[f, :, pl.ds(128 * i, 128)] for i in range(3)]
        right = [r_ref[f, :, pl.ds(128 * i, 128)] for i in range(3)]
        xa = [x_ref[pl.ds((oa * 3 + i) * 2 * cap + cap + ra, 1), :] for i in range(3)]
        xb = [x_ref[pl.ds((ob * 3 + i) * 2 * cap + cap + rb, 1), :] for i in range(3)]
        coef_b = jnp.sum(sum(right[i] * xb[i] for i in range(3)), axis=1, keepdims=True)
        coef_a = jnp.sum(sum(left[i] * xa[i] for i in range(3)), axis=1, keepdims=True)
        rank = left[0].shape[0]
        for i in range(3):
            for k, part in ((i, left[i] * coef_b), (3 + i, right[i] * coef_a)):
                at = pl.ds(pl.multiple_of((6 * f + k) * 8, 8), 8)
                sum_ref[at, :] = sum(part[8 * h : 8 * h + 8] for h in range(rank // 8))
        return 0

    lax.fori_loop(0, count, body, 0, unroll=8)

    def add_rows(q, _):
        for k in range(6):
            rows = [sum_ref[pl.ds(48 * 8 * q + 8 * k + m, 8, stride=48), :] for m in range(8)]
            row_ref[pl.ds(pl.multiple_of(k * count + 8 * q, 8), 8), :] = sum(rows)
        return 0

    lax.fori_loop(0, count // 8, add_rows, 0, unroll=2)

    def send(f, _):
        (oa, ra), (ob, rb) = ends(f)
        out_ref[pl.ds(oa * 3 * cap + ra, 3, stride=cap), :] = row_ref[pl.ds(f, 3, stride=count), :]
        out_ref[pl.ds(ob * 3 * cap + rb, 3, stride=cap), :] = row_ref[
            pl.ds(3 * count + f, 3, stride=count), :
        ]
        return 0

    lax.fori_loop(0, count, send, 0, unroll=8)


def slot_geometry(in_ref, geo_ref, *, cap):
    n = in_ref.shape[0]

    def body(d, _):
        corner = []
        for m in range(3):
            pick = in_ref[d, 3 + m].astype(jnp.int32)
            corner.append(
                [jnp.take_along_axis(in_ref[d, i], pick, axis=1) for i in range(3)]
            )
        e1 = [corner[1][i] - corner[0][i] for i in range(3)]
        e2 = [corner[2][i] - corner[0][i] for i in range(3)]
        cx = e1[1] * e2[2] - e1[2] * e2[1]
        cy = e1[2] * e2[0] - e1[0] * e2[2]
        cz = e1[0] * e2[1] - e1[1] * e2[0]
        weight = jnp.sqrt(cx * cx + cy * cy + cz * cz + area_floor) / 6.0
        for s in range(3):
            for i in range(3):
                point = sum((big if m == s else small) * corner[m][i] for m in range(3))
                geo_ref[d, pl.ds((3 * s + i) * cap, cap), :] = point
        geo_ref[d, pl.ds(9 * cap, cap), :] = weight
        return 0

    lax.fori_loop(0, n, body, 0)


def pair_ends(idx_ref, pair, count):
    return (
        (idx_ref[0, pair], idx_ref[1, pair]),
        (idx_ref[0, count + pair], idx_ref[1, count + pair]),
    )


def skew_start(idx_ref, parts, base_ref, pair, *, cap, count):
    (oa, ra), _ = pair_ends(idx_ref, pair, count)
    at = 0
    for ref, comps in parts:
        for c in range(comps):
            row = jnp.broadcast_to(ref[oa, pl.ds(c * cap + ra, 1), :], (8, 128))
            base_ref[at + c] = pltpu.roll(row, 0, 1, stride=1, stride_axis=0)
        at += comps


def skew_tile(base_ref, dst_ref, t):
    for c in range(base_ref.shape[0]):
        dst_ref[c, pl.ds(pl.multiple_of(8 * t, 8), 8), :] = pltpu.roll(base_ref[c], 8 * t, 1)


def weighted(geo_ref, x_ref, y_ref, *, cap):
    def body(d, _):
        weight = geo_ref[d, pl.ds(9 * cap, cap), :]
        for i in range(3):
            y_ref[d, pl.ds(i * cap, cap), :] = weight * x_ref[d, i, pl.ds(0, cap), :]
        return 0

    lax.fori_loop(0, x_ref.shape[0], body, 0, unroll=4)


def apply_tile(mats, ya, yb, second):
    kxx, kxy, kxz, kyy, kyz, kzz = mats
    full = ((kxx, kxy, kxz), (kxy, kyy, kyz), (kxz, kyz, kzz))
    firsts = [full[i][0] * yb[0] + full[i][1] * yb[1] + full[i][2] * yb[2] for i in range(3)]
    second = [
        second[j] + (full[0][j] * ya[0] + full[1][j] * ya[1] + full[2][j] * ya[2])
        for j in range(3)
    ]
    return firsts, second


def return_terms(idx_ref, geo_ref, first_ref, second_ref, out_ref, row_ref, *, cap, count):
    def add_rows(q, _):
        for i in range(3):
            first = second = None
            for m in range(8):
                rows = pl.ds((24 * 8) * q + 8 * i + m, 8, stride=24)
                one, two = first_ref[rows, :], second_ref[rows, :]
                first = one if m == 0 else first + pltpu.roll(one, 128 - m, 1)
                second = two if m == 0 else second + two
            row_ref[pl.ds(pl.multiple_of(i * count + 8 * q, 8), 8), :] = first
            row_ref[pl.ds(pl.multiple_of((3 + i) * count + 8 * q, 8), 8), :] = second
        return 0

    lax.fori_loop(0, count // 8, add_rows, 0)

    def body(p, _):
        (oa, ra), (ob, rb) = pair_ends(idx_ref, p, count)
        wa = geo_ref[oa, pl.ds(9 * cap + ra, 1), :]
        wb = geo_ref[ob, pl.ds(9 * cap + rb, 1), :]
        first = row_ref[pl.ds(p, 3, stride=count), :]
        second = row_ref[pl.ds(3 * count + p, 3, stride=count), :]
        out_ref[pl.ds(oa * 3 * cap + ra, 3, stride=cap), :] = wa * first
        out_ref[pl.ds(ob * 3 * cap + rb, 3, stride=cap), :] = wb * second
        return 0

    lax.fori_loop(0, count, body, 0, unroll=8)


def near_tile(col, row):
    su = sv = xx = xy = xz = yy = yz = None
    for s in range(3):
        for q in range(3):
            x = col[3 * s] - row[3 * q]
            y = col[3 * s + 1] - row[3 * q + 1]
            z = col[3 * s + 2] - row[3 * q + 2]
            u = lax.rsqrt(x * x + y * y + z * z + soft_sq)
            v = u * u * u
            vx = v * x
            vy = v * y
            if su is None:
                su, sv = u, v
                xx, xy, xz, yy, yz = vx * x, vx * y, vx * z, vy * y, vy * z
            else:
                su, sv = su + u, sv + v
                xx, xy, xz = xx + vx * x, xy + vx * y, xz + vx * z
                yy, yz = yy + vy * y, yz + vy * z
    zz = su - soft_sq * sv - xx - yy
    diag = kelvin_diag * su
    return (xx + diag, xy, xz, yy + diag, yz, zz + diag)


def sweep_pairs(
    idx_ref, parts, bases, bufs, tile_mats, sums, *, step, pair0, pairs, group, cap, count, unroll, block
):
    def some_pairs(h, _):
        for j in range(block):
            src, dst, base = bufs[j % 2], bufs[1 - j % 2], bases[j % 2]
            g = block * h + j
            local = step * group + g
            pair = pair0 + local
            following = jnp.minimum(pair + 1, pair0 + pairs - 1)
            skew_start(idx_ref, parts, base, following, cap=cap, count=count)
            _, (ob, rb) = pair_ends(idx_ref, pair, count)
            row = [
                jnp.broadcast_to(ref[ob, pl.ds(c * cap + rb, 1), :], (8, 128))
                for ref, comps in parts
                for c in range(comps)
            ]
            comps = len(row)

            def tile_body(t, carry, g=g, src=src, dst=dst, base=base, row=row):
                if sums is not None:
                    held, first, second = carry
                    back = (128 - 8 * (t - 1)) % 128
                    first = [first[i] + pltpu.roll(held[i], back, 1) for i in range(3)]
                skew_tile(base, dst, t)
                tile = pl.ds(pl.multiple_of(8 * t, 8), 8)
                col = [src[c, tile, :] for c in range(comps)]
                mats = tile_mats(g, tile, col, row)
                if sums is None:
                    return carry
                held, second = apply_tile(mats, col[comps - 3 :], row[comps - 3 :], second)
                return held, first, second

            zero = [jnp.zeros((8, 128), f32)] * 3
            start = 0 if sums is None else (zero, zero, zero)
            carry = lax.fori_loop(0, 16, tile_body, start, unroll=unroll)
            if sums is not None:
                held, first, second = carry
                for i in range(3):
                    at = pl.ds(pl.multiple_of(24 * local + 8 * i, 8), 8)
                    sums[0][at, :] = first[i] + pltpu.roll(held[i], 8, 1)
                    sums[1][at, :] = second[i]
        return 0

    lax.fori_loop(0, group // block, some_pairs, 0)


def skew_first_pair(idx_ref, parts, base, buf, pair, *, cap, count):
    skew_start(idx_ref, parts, base, pair, cap=cap, count=count)

    def body(t, _):
        skew_tile(base, buf, t)
        return 0

    lax.fori_loop(0, 16, body, 0, unroll=4)


def build_blocks(idx_ref, geo_ref, k_ref, base0, base1, buf0, buf1, *, pair0, pairs, cap, count):
    step = pl.program_id(0)
    parts = ((geo_ref, 9),)

    @pl.when(step == 0)
    def _():
        skew_first_pair(idx_ref, parts, base1, buf0, pair0, cap=cap, count=count)

    def tile_mats(g, tile, col, row):
        mats = near_tile(col, row)
        for m in range(6):
            k_ref[g, m, tile, :] = mats[m]
        return mats

    sweep_pairs(
        idx_ref, parts, (base0, base1), (buf0, buf1), tile_mats, None,
        step=step, pair0=pair0, pairs=pairs, group=k_ref.shape[0], cap=cap, count=count,
        unroll=BUILD_UNROLL, block=2,
    )


def build_kernel(idx_ref, in_ref, k_ref, geo_ref, *skews, pairs, cap, count):
    @pl.when(pl.program_id(0) == 0)
    def _():
        slot_geometry(in_ref, geo_ref, cap=cap)

    build_blocks(idx_ref, geo_ref, k_ref, *skews, pair0=0, pairs=pairs, cap=cap, count=count)


def build_rest_kernel(idx_ref, geo_ref, old_ref, far_ref, k_ref, *skews, pair0, cap, count):
    build_blocks(
        idx_ref, geo_ref, k_ref, *skews, pair0=pair0, pairs=count - pair0, cap=cap, count=count
    )


def apply_kernel(
    idx_ref, geo_ref, x_ref, k_ref, out_ref,
    first_ref, second_ref, row_ref, y_ref, base0, base1, buf0, buf1, *, cap, count,
):
    step = pl.program_id(0)
    parts = ((y_ref, 3),)

    @pl.when(step == 0)
    def _():
        weighted(geo_ref, x_ref, y_ref, cap=cap)
        skew_first_pair(idx_ref, parts, base1, buf0, 0, cap=cap, count=count)

    def tile_mats(g, tile, col, row):
        return [k_ref[g, m, tile, :] for m in range(6)]

    sweep_pairs(
        idx_ref, parts, (base0, base1), (buf0, buf1), tile_mats, (first_ref, second_ref),
        step=step, pair0=0, pairs=count, group=k_ref.shape[0], cap=cap, count=count,
        unroll=APPLY_UNROLL, block=4,
    )

    @pl.when(step == pl.num_programs(0) - 1)
    def _():
        return_terms(
            idx_ref, geo_ref, first_ref, second_ref, out_ref, row_ref, cap=cap, count=count
        )


def add_up(ask_ref, near_ref, far_ref, accs, out_ref, *, n, cap):
    clusters = out_ref.shape[1]
    for acc in accs:
        acc[...] = jnp.zeros(acc.shape, f32)

    def body(d, _):
        for s in range(cap):
            for part, ref in enumerate((near_ref, far_ref)):
                acc = accs[2 * part + s % 2]
                at = pl.ds(pl.multiple_of(8 * ask_ref[d, part * cap + s], 8), 3)
                acc[at, :] += ref[pl.ds(d * 3 * cap + s, 3, stride=cap), :]
        return 0

    lax.fori_loop(0, n, body, 0)

    def total(q, _):
        at = pl.ds(pl.multiple_of(64 * q, 64), 64)
        accs[0][at, :] = (accs[0][at, :] + accs[1][at, :]) + (accs[2][at, :] + accs[3][at, :])
        for i in range(3):
            out_ref[i, pl.ds(pl.multiple_of(8 * q, 8), 8), :] = accs[0][
                pl.ds(64 * q + i, 8, stride=8), :
            ]
        return 0

    lax.fori_loop(0, clusters // 8, total, 0)


def merge_kernel(ask_ref, rn_ref, rf_ref, out_ref, pack_ref, *accs, n, cap):
    add_up(ask_ref, rn_ref, rf_ref, accs, out_ref, n=n, cap=cap)
    last = out_ref.shape[1] - 1

    def fetch(c):
        return [accs[0][pl.ds(pl.multiple_of(8 * jnp.minimum(c, last), 8), 3), :]]

    pack_rows(ask_ref, fetch, pack_ref, n=n, slots=2 * cap, kinds=1)


PRODUCTS = ((0, 0), (0, 1), (1, 1), (0, 2), (1, 2), (2, 2))


def gram_kernel(ask_ref, rn_ref, rf_ref, v0_ref, v1_ref, out_ref, part_ref, *accs, n, cap):
    add_up(ask_ref, rn_ref, rf_ref, accs, out_ref, n=n, cap=cap)
    clusters = out_ref.shape[1]
    refs = (v0_ref, v1_ref, out_ref)
    zero = jnp.zeros((8, 128), f32)
    totals = [(zero, zero)] * 6
    for i in range(3):

        def body(t, totals):
            tiles = [ref[i, pl.ds(8 * t, 8), :] for ref in refs]
            halves = [split(tile) for tile in tiles]
            new = []
            for k, (a, b) in enumerate(PRODUCTS):
                (ah, al), (bh, bl) = halves[a], halves[b]
                p = tiles[a] * tiles[b]
                e = ((ah * bh - p) + ah * bl + al * bh) + al * bl
                hi, lo = totals[k]
                s, err = two_sum(hi, p)
                new.append((s, lo + (err + e)))
            return new

        totals = lax.fori_loop(0, clusters // 8, body, totals)
    hi = jnp.concatenate([t[0] for t in totals], axis=0)
    lo = jnp.concatenate([t[1] for t in totals], axis=0)
    for shift in (64, 32, 16, 8, 4, 2, 1):
        hi, lo = dd_add((hi, lo), (pltpu.roll(hi, shift, 1), pltpu.roll(lo, shift, 1)))
    lane = lax.broadcasted_iota(jnp.int32, (8, 128), 1)
    shi = slo = zero
    for k in range(6):
        shi = jnp.where(lane == k, hi[8 * k : 8 * k + 8], shi)
        slo = jnp.where(lane == k, lo[8 * k : 8 * k + 8], slo)
    for shift in (4, 2, 1):
        shi, slo = dd_add((shi, slo), (pltpu.roll(shi, shift, 0), pltpu.roll(slo, shift, 0)))
    packed = jnp.where(lane < 8, shi, pltpu.roll(slo, 8, 1))
    part_ref[...] = jnp.broadcast_to(packed[0:1, :], part_ref.shape)


def final_kernel(part_ref, v0_ref, v1_ref, v2_ref, basis_ref, hess_ref, *, size_all):
    hi = part_ref[...]
    lo = pltpu.roll(hi, 120, 1)
    rows = hi.shape[0]
    while rows > 1:
        half = rows // 2
        hi, lo = dd_add((hi[:half], lo[:half]), (hi[half:], lo[half:]))
        rows = half
    inv = 1.0 / size_all
    hi, lo = dd_scale((hi, lo), jnp.full(hi.shape, inv, f32)) if size_all & (size_all - 1) == 0 else dd_div_const(hi, lo, size_all)
    g = [(hi[:, k : k + 1], lo[:, k : k + 1]) for k in range(6)]
    g00, g01, g11, g02, g12, g22 = g
    eps = jnp.full((1, 1), norm_eps, f32)
    none = jnp.zeros((1, 1), f32)
    s2 = dd_add(g00, (eps, none))
    s = jnp.sqrt(s2[0])
    p = g01[0] / s2[0]
    r1 = dd_add(g11, dd_scale(dd_add(dd_scale(g00, p), dd_scale(g01, none - 2.0)), p))
    nf = jnp.sqrt(jnp.maximum(r1[0], 0.0) / s2[0] + norm_eps)
    snf = s * nf
    c0 = dd_add(g02, dd_scale(g01, -p))
    pc = c0[0] / (s2[0] * nf)
    c1 = dd_add(dd_add(g12, dd_scale(g11, -p)), dd_scale(c0, -p))
    ps = c1[0] / (s2[0] * nf * nf)
    a1 = -(p + ps)
    a0 = ps * p - pc * nf
    t2 = dd_add(g22, dd_scale(dd_add(dd_scale(g12, a1), dd_scale(g02, a0)), none + 2.0))
    t1 = dd_scale(dd_add(dd_scale(g11, a1), dd_scale(g01, 2.0 * a0)), a1)
    t0 = dd_scale(dd_scale(g00, a0), a0)
    w2 = dd_add(dd_add(t2, t1), t0)
    n2 = jnp.sqrt(jnp.maximum(w2[0], 0.0) / (snf * snf) + norm_eps)
    k1 = 1.0 / snf
    k2 = 1.0 / (snf * n2)
    for i in range(3):
        v0, v1, v2 = v0_ref[i], v1_ref[i], v2_ref[i]
        basis_ref[0, i] = (v1 - p * v0) * k1
        basis_ref[1, i] = (v2 + a1 * v1 + a0 * v0) * k2
    top = jnp.concatenate([p, nf, none], axis=1)
    bottom = jnp.concatenate([pc, ps, n2], axis=1)
    hess_ref[...] = jnp.concatenate([top, bottom], axis=0)


def dd_div_const(hi, lo, size_all):
    d = jnp.full(hi.shape, float(size_all), f32)
    q = hi / d
    p, e = two_prod(q, d)
    rest = ((hi - p) - e) + lo
    return q, rest / d


def per_device(
    right_side, vertices, panels, near_owner, near_local, far_owner, far_local, far_left, far_right
):
    n = lax.axis_size("dev")
    clusters, _, width = right_side.shape
    near_count = near_owner.shape[0]
    far_count = far_owner.shape[0]
    cap = max(2, 4 * near_count // n)
    size_all = clusters * n * 3 * width
    x0 = right_side.transpose(1, 0, 2)
    shape = jax.ShapeDtypeStruct

    def exchange(block):
        return lax.all_to_all(block, "dev", split_axis=0, concat_axis=0, tiled=True)

    slots = max(128, 2 * cap)
    ask, idx = pl.pallas_call(
        lambda *refs: prep_kernel(*refs, cap=cap, trash=clusters),
        out_shape=(shape((n, slots), jnp.int32), shape((8, 2 * near_count), jnp.int32)),
        compiler_params=params(60),
        name="prep",
    )(near_owner.T, near_local.T, far_owner.T, far_local.T)
    asked = exchange(ask)

    rows3 = shape((n * 3 * cap, width), f32)
    both = shape((n * 6 * cap, width), f32)

    def flat(array):
        return array.reshape(-1, width)

    near_out = (
        pl.pallas_call(
            lambda *refs: pack_near_kernel(*refs, n=n, slots=cap),
            out_shape=shape((n * 6 * cap, width), f32),
            in_specs=[SM, VM, VM],
            scratch_shapes=[pltpu.VMEM((3 * clusters, width), f32)],
            compiler_params=params(60),
            cost_estimate=cost(4.0),
            name="pack_near",
        )(asked, flat(vertices.transpose(1, 0, 2)), flat(panels.transpose(1, 0, 2)))
    )
    near_in = exchange(near_out)
    x0_out = pl.pallas_call(
        lambda *refs: pack_kernel(*refs, n=n, slots=2 * cap),
        out_shape=both,
        in_specs=[SM, VM],
        compiler_params=params(),
        cost_estimate=cost(3.0),
        name="pack",
    )(asked, flat(x0))
    x0_in = exchange(x0_out)

    group = 8
    early = near_count // 2
    k_block = (group, 6, width, width)
    k_shape = shape((near_count, 6, width, width), f32)
    rows10 = (n, 10 * cap, width)

    def whole(*dims):
        return pl.BlockSpec(dims, lambda g: (0,) * len(dims))

    def skews(comps):
        return [pltpu.VMEM((comps, 8, width), f32)] * 2 + [
            pltpu.VMEM((comps, width, width), f32)
        ] * 2

    stored, geometry = pl.pallas_call(
        lambda *refs: build_kernel(*refs, pairs=early, cap=cap, count=near_count),
        out_shape=(k_shape, shape(rows10, f32)),
        grid=(early // group,),
        in_specs=[SM, whole(n, 6, cap, width)],
        out_specs=(pl.BlockSpec(k_block, lambda g: (g, 0, 0, 0)), whole(*rows10)),
        scratch_shapes=skews(9),
        compiler_params=params(44),
        cost_estimate=cost(30.0),
        name="build",
    )(idx, near_in.reshape(n, 6, cap, width))

    def far_product(received):
        return pl.pallas_call(
            lambda *refs: far_kernel(*refs, cap=cap),
            out_shape=rows3,
            in_specs=[SM, VM, VM, VM],
            scratch_shapes=[
                pltpu.VMEM((far_count * 48, width), f32),
                pltpu.VMEM((6 * far_count, width), f32),
            ],
            compiler_params=params(8),
            cost_estimate=cost(5.0),
            name="far",
        )(idx, received, far_left, far_right)

    far_terms = far_product(x0_in)
    far_back = exchange(far_terms)
    stored = pl.pallas_call(
        lambda *refs: build_rest_kernel(*refs, pair0=early, cap=cap, count=near_count),
        out_shape=k_shape,
        grid=((near_count - early) // group,),
        in_specs=[SM, whole(*rows10), ANY, ANY],
        out_specs=pl.BlockSpec(k_block, lambda g: (g + early // group, 0, 0, 0)),
        scratch_shapes=skews(9),
        input_output_aliases={2: 0},
        compiler_params=params(44),
        cost_estimate=cost(30.0),
        name="build_rest",
    )(idx, geometry, stored, far_terms)

    def apply_stored(received):
        return (
            pl.pallas_call(
                lambda *refs: apply_kernel(*refs, cap=cap, count=near_count),
                out_shape=rows3,
                grid=(near_count // group,),
                in_specs=[
                    SM,
                    whole(*rows10),
                    whole(n, 3, 2 * cap, width),
                    pl.BlockSpec(k_block, lambda g: (g, 0, 0, 0)),
                ],
                out_specs=whole(*rows3.shape),
                scratch_shapes=[pltpu.VMEM((near_count * 24, width), f32)] * 2
                + [pltpu.VMEM((6 * near_count, width), f32)]
                + [pltpu.VMEM((n, 3 * cap, width), f32)]
                + skews(3),
                compiler_params=params(44),
                cost_estimate=cost(18.0),
                name="apply",
            )(idx, geometry, received.reshape(n, 3, 2 * cap, width), stored)
        )

    near_terms = apply_stored(x0_in)
    near_back = exchange(near_terms)

    accs = [pltpu.VMEM(((clusters + 1) * 8, width), f32)] * 4
    x1, x1_out = pl.pallas_call(
        lambda *refs: merge_kernel(*refs, n=n, cap=cap),
        out_shape=(shape((3, clusters, width), f32), both),
        in_specs=[SM, VM, VM],
        scratch_shapes=accs,
        compiler_params=params(),
        cost_estimate=cost(5.0),
        name="merge",
    )(asked, near_back, far_back)
    x1_in = exchange(x1_out)
    far_terms2 = far_product(x1_in)
    far_back2 = exchange(far_terms2)
    near_terms2 = apply_stored(x1_in)
    near_back2 = exchange(near_terms2)

    x2, part = pl.pallas_call(
        lambda *refs: gram_kernel(*refs, n=n, cap=cap),
        out_shape=(shape((3, clusters, width), f32), shape((n, 128), f32)),
        in_specs=[SM, VM, VM, VM, VM],
        scratch_shapes=accs,
        compiler_params=params(),
        cost_estimate=cost(5.0),
        name="gram",
    )(asked, near_back2, far_back2, x0, x1)
    parts = exchange(part)
    basis, hess = pl.pallas_call(
        lambda *refs: final_kernel(*refs, size_all=size_all),
        out_shape=(shape((2, 3, clusters, width), f32), shape((2, 3), f32)),
        compiler_params=params(),
        name="final",
    )(parts, x0, x1, x2)
    return (basis.transpose(0, 2, 1, 3), hess.T)


def solution(mesh):
    per_cluster = P("dev", None, None)
    per_pair = P("dev", None)
    in_specs = (per_cluster,) * 3 + (per_pair,) * 4 + (per_cluster,) * 2
    out_specs = (P(None, "dev", None, None), P())

    return jax.shard_map(
        per_device, mesh=mesh, in_specs=in_specs, out_specs=out_specs, check_vma=False
    )
```

```python
import jax
import jax.numpy as jnp
from jax import lax
from jax.experimental import pallas as pl
from jax.experimental.pallas import tpu as pltpu
from jax.sharding import PartitionSpec as P


soft_sq = 0.0025
area_floor = 6.25e-06
kelvin_diag = 1.8
norm_eps = 1e-06
big = 2.0 / 3.0
small = 1.0 / 6.0
BUILD_UNROLL = 4
APPLY_UNROLL = 16
f32 = jnp.float32
VM = pl.BlockSpec(memory_space=pltpu.VMEM)
SM = pl.BlockSpec(memory_space=pltpu.SMEM)


def params(mib=8):
    return pltpu.CompilerParams(vmem_limit_bytes=mib << 20)


def cost(us):
    return pl.CostEstimate(flops=0, transcendentals=0, bytes_accessed=int(us * 3.0e6))


def two_sum(a, b):
    s = a + b
    t = s - a
    return s, (a - (s - t)) + (b - t)


def split(a):
    c = a * 4097.0
    hi = c - (c - a)
    return hi, a - hi


def two_prod(a, b):
    p = a * b
    ah, al = split(a)
    bh, bl = split(b)
    return p, ((ah * bh - p) + ah * bl + al * bh) + al * bl


def dd_add(x, y):
    s, e = two_sum(x[0], y[0])
    e = e + (x[1] + y[1])
    hi = s + e
    return hi, e - (hi - s)


def dd_scale(x, f):
    p, e = two_prod(x[0], f)
    e = e + x[1] * f
    hi = p + e
    return hi, e - (hi - p)


def prep_kernel(no_ref, nl_ref, fo_ref, fl_ref, ask_ref, idx_ref, *, cap, trash):
    n = ask_ref.shape[0]
    width = 2 * no_ref.shape[1]
    ask = jnp.full(ask_ref.shape, float(trash), f32)
    rows = []
    for part, (o_ref, l_ref) in enumerate(((no_ref, nl_ref), (fo_ref, fl_ref))):
        owner = jnp.concatenate([o_ref[0:1, :], o_ref[1:2, :]], axis=1).astype(f32)
        local = jnp.concatenate([l_ref[0:1, :], l_ref[1:2, :]], axis=1).astype(f32)
        across = jnp.broadcast_to(owner, (width, width))
        down = across.T
        row = lax.broadcasted_iota(jnp.int32, (width, width), 0)
        col = lax.broadcasted_iota(jnp.int32, (width, width), 1)
        earlier = jnp.where((across == down) & (row < col), 1.0, 0.0)
        rank = jnp.sum(earlier, axis=0, keepdims=True)
        dest = lax.broadcasted_iota(jnp.int32, (n, width), 0).astype(f32)
        lhs = jnp.where(dest == owner, local + 1.0, 0.0).astype(jnp.bfloat16)
        slot = lax.broadcasted_iota(jnp.int32, (ask_ref.shape[1], width), 0).astype(f32)
        rhs = jnp.where(slot == rank + float(part * cap), 1.0, 0.0).astype(jnp.bfloat16)
        found = lax.dot_general(
            lhs, rhs, (((1,), (1,)), ((), ())), preferred_element_type=f32
        )
        ask = jnp.where(found > 0.5, found - 1.0, ask)
        rows += [owner, rank]
    ask_ref[...] = ask.astype(jnp.int32)
    idx_ref[...] = jnp.concatenate(rows + rows, axis=0).astype(jnp.int32)


def pack_rows(ask_ref, fetch, out_ref, *, n, slots, kinds):
    def body(d, _):
        for s in range(slots):
            rows = fetch(ask_ref[d, s])
            for k in range(kinds):
                at = (d * kinds + k) * 3 * slots + s
                out_ref[pl.ds(at, 3, stride=slots), :] = rows[k]
        return 0

    lax.fori_loop(0, n, body, 0, unroll=2)


def cluster_rows(refs):
    clusters = refs[0].shape[0] // 3

    def fetch(c):
        c = jnp.minimum(c, clusters - 1)
        return [ref[pl.ds(c, 3, stride=clusters), :] for ref in refs]

    return fetch


def pack_kernel(ask_ref, x_ref, out_ref, *, n, slots):
    pack_rows(ask_ref, cluster_rows((x_ref,)), out_ref, n=n, slots=slots, kinds=1)


def pack_near_kernel(ask_ref, v_ref, p_ref, out_ref, pan_ref, *, n, slots):
    pan_ref[...] = p_ref[...].astype(f32)
    pack_rows(ask_ref, cluster_rows((v_ref, pan_ref)), out_ref, n=n, slots=slots, kinds=2)


def far_kernel(idx_ref, x_ref, l_ref, r_ref, out_ref, sum_ref, row_ref, *, cap):
    count = l_ref.shape[0]

    def ends(f):
        oa, ra = idx_ref[2, f], idx_ref[3, f]
        ob, rb = idx_ref[2, count + f], idx_ref[3, count + f]
        return (oa, ra), (ob, rb)

    def body(f, _):
        (oa, ra), (ob, rb) = ends(f)
        left = [l_ref[f, :, pl.ds(128 * i, 128)] for i in range(3)]
        right = [r_ref[f, :, pl.ds(128 * i, 128)] for i in range(3)]
        xa = [x_ref[pl.ds((oa * 3 + i) * 2 * cap + cap + ra, 1), :] for i in range(3)]
        xb = [x_ref[pl.ds((ob * 3 + i) * 2 * cap + cap + rb, 1), :] for i in range(3)]
        coef_b = jnp.sum(sum(right[i] * xb[i] for i in range(3)), axis=1, keepdims=True)
        coef_a = jnp.sum(sum(left[i] * xa[i] for i in range(3)), axis=1, keepdims=True)
        rank = left[0].shape[0]
        for i in range(3):
            for k, term in ((i, left[i] * coef_b), (3 + i, right[i] * coef_a)):
                at = pl.ds(pl.multiple_of((6 * f + k) * 8, 8), 8)
                sum_ref[at, :] = sum(term[8 * h : 8 * h + 8] for h in range(rank // 8))
        return 0

    lax.fori_loop(0, count, body, 0, unroll=8)

    def add_rows(q, _):
        for k in range(6):
            rows = [sum_ref[pl.ds(48 * 8 * q + 8 * k + m, 8, stride=48), :] for m in range(8)]
            row_ref[pl.ds(pl.multiple_of(k * count + 8 * q, 8), 8), :] = sum(rows)
        return 0

    lax.fori_loop(0, count // 8, add_rows, 0, unroll=2)

    def send(f, _):
        (oa, ra), (ob, rb) = ends(f)
        out_ref[pl.ds(oa * 3 * cap + ra, 3, stride=cap), :] = row_ref[pl.ds(f, 3, stride=count), :]
        out_ref[pl.ds(ob * 3 * cap + rb, 3, stride=cap), :] = row_ref[
            pl.ds(3 * count + f, 3, stride=count), :
        ]
        return 0

    lax.fori_loop(0, count, send, 0, unroll=8)


def slot_geometry(in_ref, geo_ref, w_ref, *, cap):
    n = in_ref.shape[0]

    def body(d, _):
        corner = []
        for m in range(3):
            pick = in_ref[d, 3 + m].astype(jnp.int32)
            corner.append(
                [jnp.take_along_axis(in_ref[d, i], pick, axis=1) for i in range(3)]
            )
        e1 = [corner[1][i] - corner[0][i] for i in range(3)]
        e2 = [corner[2][i] - corner[0][i] for i in range(3)]
        cx = e1[1] * e2[2] - e1[2] * e2[1]
        cy = e1[2] * e2[0] - e1[0] * e2[2]
        cz = e1[0] * e2[1] - e1[1] * e2[0]
        weight = jnp.sqrt(cx * cx + cy * cy + cz * cz + area_floor) / 6.0
        for s in range(3):
            for i in range(3):
                point = sum((big if m == s else small) * corner[m][i] for m in range(3))
                geo_ref[d, pl.ds((3 * s + i) * cap, cap), :] = point
        w_ref[d] = weight
        return 0

    lax.fori_loop(0, n, body, 0)


def pair_ends(idx_ref, pair, count):
    return (
        (idx_ref[0, pair], idx_ref[1, pair]),
        (idx_ref[0, count + pair], idx_ref[1, count + pair]),
    )


def skew_start(idx_ref, parts, base_ref, pair, *, cap, count):
    (oa, ra), _ = pair_ends(idx_ref, pair, count)
    at = 0
    for ref, comps in parts:
        for c in range(comps):
            row = jnp.broadcast_to(ref[oa, pl.ds(c * cap + ra, 1), :], (8, 128))
            base_ref[at + c] = pltpu.roll(row, 0, 1, stride=1, stride_axis=0)
        at += comps


def skew_tile(base_ref, dst_ref, t):
    for c in range(base_ref.shape[0]):
        dst_ref[c, pl.ds(pl.multiple_of(8 * t, 8), 8), :] = pltpu.roll(base_ref[c], 8 * t, 1)


def weighted(w_ref, x_ref, y_ref, *, cap):
    def body(d, _):
        for i in range(3):
            y_ref[d, pl.ds(i * cap, cap), :] = w_ref[d] * x_ref[d, i, pl.ds(0, cap), :]
        return 0

    lax.fori_loop(0, x_ref.shape[0], body, 0, unroll=4)


def apply_tile(mats, ya, yb, second):
    kxx, kxy, kxz, kyy, kyz, kzz = mats
    full = ((kxx, kxy, kxz), (kxy, kyy, kyz), (kxz, kyz, kzz))
    firsts = [full[i][0] * yb[0] + full[i][1] * yb[1] + full[i][2] * yb[2] for i in range(3)]
    second = [
        second[j] + (full[0][j] * ya[0] + full[1][j] * ya[1] + full[2][j] * ya[2])
        for j in range(3)
    ]
    return firsts, second


def return_terms(idx_ref, w_ref, first_ref, second_ref, out_ref, row_ref, *, cap, count):
    def add_rows(q, _):
        for i in range(3):
            first = second = None
            for m in range(8):
                rows = pl.ds((24 * 8) * q + 8 * i + m, 8, stride=24)
                one, two = first_ref[rows, :], second_ref[rows, :]
                first = one if m == 0 else first + pltpu.roll(one, 128 - m, 1)
                second = two if m == 0 else second + two
            row_ref[pl.ds(pl.multiple_of(i * count + 8 * q, 8), 8), :] = first
            row_ref[pl.ds(pl.multiple_of((3 + i) * count + 8 * q, 8), 8), :] = second
        return 0

    lax.fori_loop(0, count // 8, add_rows, 0)

    def body(p, _):
        (oa, ra), (ob, rb) = pair_ends(idx_ref, p, count)
        wa = w_ref[oa, pl.ds(ra, 1), :]
        wb = w_ref[ob, pl.ds(rb, 1), :]
        first = row_ref[pl.ds(p, 3, stride=count), :]
        second = row_ref[pl.ds(3 * count + p, 3, stride=count), :]
        out_ref[pl.ds(oa * 3 * cap + ra, 3, stride=cap), :] = wa * first
        out_ref[pl.ds(ob * 3 * cap + rb, 3, stride=cap), :] = wb * second
        return 0

    lax.fori_loop(0, count, body, 0, unroll=8)


def near_tile(col, row):
    su = sv = xx = xy = xz = yy = yz = None
    for s in range(3):
        for q in range(3):
            x = col[3 * s] - row[3 * q]
            y = col[3 * s + 1] - row[3 * q + 1]
            z = col[3 * s + 2] - row[3 * q + 2]
            u = lax.rsqrt(x * x + y * y + z * z + soft_sq)
            v = u * u * u
            vx = v * x
            vy = v * y
            if su is None:
                su, sv = u, v
                xx, xy, xz, yy, yz = vx * x, vx * y, vx * z, vy * y, vy * z
            else:
                su, sv = su + u, sv + v
                xx, xy, xz = xx + vx * x, xy + vx * y, xz + vx * z
                yy, yz = yy + vy * y, yz + vy * z
    zz = su - soft_sq * sv - xx - yy
    diag = kelvin_diag * su
    return (xx + diag, xy, xz, yy + diag, yz, zz + diag)


def sweep_pairs(
    idx_ref, parts, bases, bufs, tile_mats, sums, *, step, pairs, group, cap, count, unroll, block
):
    def some_pairs(h, _):
        for j in range(block):
            src, dst, base = bufs[j % 2], bufs[1 - j % 2], bases[j % 2]
            g = block * h + j
            local = step * group + g
            pair = local
            following = jnp.minimum(pair + 1, pairs - 1)
            skew_start(idx_ref, parts, base, following, cap=cap, count=count)
            _, (ob, rb) = pair_ends(idx_ref, pair, count)
            row = [
                jnp.broadcast_to(ref[ob, pl.ds(c * cap + rb, 1), :], (8, 128))
                for ref, comps in parts
                for c in range(comps)
            ]
            comps = len(row)

            def tile_body(t, carry, g=g, src=src, dst=dst, base=base, row=row):
                if sums is not None:
                    held, first, second = carry
                    back = (128 - 8 * (t - 1)) % 128
                    first = [first[i] + pltpu.roll(held[i], back, 1) for i in range(3)]
                skew_tile(base, dst, t)
                tile = pl.ds(pl.multiple_of(8 * t, 8), 8)
                col = [src[c, tile, :] for c in range(comps)]
                mats = tile_mats(g, tile, col, row)
                if sums is None:
                    return carry
                held, second = apply_tile(mats, col[comps - 3 :], row[comps - 3 :], second)
                return held, first, second

            zero = [jnp.zeros((8, 128), f32)] * 3
            start = 0 if sums is None else (zero, zero, zero)
            carry = lax.fori_loop(0, 16, tile_body, start, unroll=unroll)
            if sums is not None:
                held, first, second = carry
                for i in range(3):
                    at = pl.ds(pl.multiple_of(24 * local + 8 * i, 8), 8)
                    sums[0][at, :] = first[i] + pltpu.roll(held[i], 8, 1)
                    sums[1][at, :] = second[i]
        return 0

    lax.fori_loop(0, group // block, some_pairs, 0)


def skew_first_pair(idx_ref, parts, base, buf, pair, *, cap, count):
    skew_start(idx_ref, parts, base, pair, cap=cap, count=count)

    def body(t, _):
        skew_tile(base, buf, t)
        return 0

    lax.fori_loop(0, 16, body, 0, unroll=4)


def build_kernel(idx_ref, in_ref, k_ref, w_ref, geo_ref, base0, base1, buf0, buf1, *, cap, count):
    step = pl.program_id(0)
    parts = ((geo_ref, 9),)

    @pl.when(step == 0)
    def _():
        slot_geometry(in_ref, geo_ref, w_ref, cap=cap)
        skew_first_pair(idx_ref, parts, base1, buf0, 0, cap=cap, count=count)

    def tile_mats(g, tile, col, row):
        mats = near_tile(col, row)
        for m in range(6):
            k_ref[g, m, tile, :] = mats[m]
        return mats

    sweep_pairs(
        idx_ref, parts, (base0, base1), (buf0, buf1), tile_mats, None,
        step=step, pairs=count, group=k_ref.shape[0], cap=cap, count=count,
        unroll=BUILD_UNROLL, block=2,
    )


def apply_kernel(
    idx_ref, w_ref, x_ref, k_hbm, out_ref,
    first_ref, second_ref, row_ref, y_ref, k_ref, sems, base0, base1, buf0, buf1, *, cap, count,
):
    depth, part = k_ref.shape[:2]
    groups = count // part
    parts = ((y_ref, 3),)

    def fetch(q, slot):
        return pltpu.make_async_copy(k_hbm.at[pl.ds(q * part, part)], k_ref.at[slot], sems.at[slot])

    for q in range(min(depth, groups)):
        fetch(q, q).start()
    weighted(w_ref, x_ref, y_ref, cap=cap)
    skew_first_pair(idx_ref, parts, base1, buf0, 0, cap=cap, count=count)

    def body(q, _):
        slot = lax.rem(q, depth)
        fetch(q, slot).wait()

        def tile_mats(g, tile, col, row):
            return [k_ref[slot, g, m, tile, :] for m in range(6)]

        sweep_pairs(
            idx_ref, parts, (base0, base1), (buf0, buf1), tile_mats, (first_ref, second_ref),
            step=q, pairs=count, group=part, cap=cap, count=count,
            unroll=APPLY_UNROLL, block=part,
        )

        @pl.when(q + depth < groups)
        def _():
            fetch(q + depth, slot).start()

        return 0

    lax.fori_loop(0, groups, body, 0)
    return_terms(idx_ref, w_ref, first_ref, second_ref, out_ref, row_ref, cap=cap, count=count)


def add_up(ask_ref, near_ref, far_ref, accs, out_ref, *, n, cap):
    clusters = out_ref.shape[1]
    for acc in accs:
        acc[...] = jnp.zeros(acc.shape, f32)

    def body(d, _):
        for s in range(cap):
            for part, ref in enumerate((near_ref, far_ref)):
                acc = accs[2 * part + s % 2]
                at = pl.ds(pl.multiple_of(8 * ask_ref[d, part * cap + s], 8), 3)
                acc[at, :] += ref[pl.ds(d * 3 * cap + s, 3, stride=cap), :]
        return 0

    lax.fori_loop(0, n, body, 0)

    def total(q, _):
        at = pl.ds(pl.multiple_of(64 * q, 64), 64)
        accs[0][at, :] = (accs[0][at, :] + accs[1][at, :]) + (accs[2][at, :] + accs[3][at, :])
        for i in range(3):
            out_ref[i, pl.ds(pl.multiple_of(8 * q, 8), 8), :] = accs[0][
                pl.ds(64 * q + i, 8, stride=8), :
            ]
        return 0

    lax.fori_loop(0, clusters // 8, total, 0)


def merge_kernel(ask_ref, rn_ref, rf_ref, out_ref, pack_ref, *accs, n, cap):
    add_up(ask_ref, rn_ref, rf_ref, accs, out_ref, n=n, cap=cap)
    last = out_ref.shape[1] - 1

    def fetch(c):
        return [accs[0][pl.ds(pl.multiple_of(8 * jnp.minimum(c, last), 8), 3), :]]

    pack_rows(ask_ref, fetch, pack_ref, n=n, slots=2 * cap, kinds=1)


PRODUCTS = ((0, 0), (0, 1), (1, 1), (0, 2), (1, 2), (2, 2))


def gram_kernel(ask_ref, rn_ref, rf_ref, v0_ref, v1_ref, out_ref, part_ref, *accs, n, cap):
    add_up(ask_ref, rn_ref, rf_ref, accs, out_ref, n=n, cap=cap)
    clusters = out_ref.shape[1]
    refs = (v0_ref, v1_ref, out_ref)
    zero = jnp.zeros((8, 128), f32)
    totals = [(zero, zero)] * 6
    for i in range(3):

        def body(t, totals):
            tiles = [ref[i, pl.ds(8 * t, 8), :] for ref in refs]
            halves = [split(tile) for tile in tiles]
            new = []
            for k, (a, b) in enumerate(PRODUCTS):
                (ah, al), (bh, bl) = halves[a], halves[b]
                p = tiles[a] * tiles[b]
                e = ((ah * bh - p) + ah * bl + al * bh) + al * bl
                hi, lo = totals[k]
                s, err = two_sum(hi, p)
                new.append((s, lo + (err + e)))
            return new

        totals = lax.fori_loop(0, clusters // 8, body, totals)
    hi = jnp.concatenate([t[0] for t in totals], axis=0)
    lo = jnp.concatenate([t[1] for t in totals], axis=0)
    for shift in (64, 32, 16, 8, 4, 2, 1):
        hi, lo = dd_add((hi, lo), (pltpu.roll(hi, shift, 1), pltpu.roll(lo, shift, 1)))
    lane = lax.broadcasted_iota(jnp.int32, (8, 128), 1)
    shi = slo = zero
    for k in range(6):
        shi = jnp.where(lane == k, hi[8 * k : 8 * k + 8], shi)
        slo = jnp.where(lane == k, lo[8 * k : 8 * k + 8], slo)
    for shift in (4, 2, 1):
        shi, slo = dd_add((shi, slo), (pltpu.roll(shi, shift, 0), pltpu.roll(slo, shift, 0)))
    packed = jnp.where(lane < 8, shi, pltpu.roll(slo, 8, 1))
    part_ref[...] = jnp.broadcast_to(packed[0:1, :], part_ref.shape)


def final_kernel(part_ref, v0_ref, v1_ref, v2_ref, basis_ref, hess_ref, *, size_all):
    hi = part_ref[...]
    lo = pltpu.roll(hi, 120, 1)
    rows = hi.shape[0]
    while rows > 1:
        half = rows // 2
        hi, lo = dd_add((hi[:half], lo[:half]), (hi[half:], lo[half:]))
        rows = half
    inv = 1.0 / size_all
    hi, lo = dd_scale((hi, lo), jnp.full(hi.shape, inv, f32)) if size_all & (size_all - 1) == 0 else dd_div_const(hi, lo, size_all)
    g = [(hi[:, k : k + 1], lo[:, k : k + 1]) for k in range(6)]
    g00, g01, g11, g02, g12, g22 = g
    eps = jnp.full((1, 1), norm_eps, f32)
    none = jnp.zeros((1, 1), f32)
    s2 = dd_add(g00, (eps, none))
    s = jnp.sqrt(s2[0])
    p = g01[0] / s2[0]
    r1 = dd_add(g11, dd_scale(dd_add(dd_scale(g00, p), dd_scale(g01, none - 2.0)), p))
    nf = jnp.sqrt(jnp.maximum(r1[0], 0.0) / s2[0] + norm_eps)
    snf = s * nf
    c0 = dd_add(g02, dd_scale(g01, -p))
    pc = c0[0] / (s2[0] * nf)
    c1 = dd_add(dd_add(g12, dd_scale(g11, -p)), dd_scale(c0, -p))
    ps = c1[0] / (s2[0] * nf * nf)
    a1 = -(p + ps)
    a0 = ps * p - pc * nf
    t2 = dd_add(g22, dd_scale(dd_add(dd_scale(g12, a1), dd_scale(g02, a0)), none + 2.0))
    t1 = dd_scale(dd_add(dd_scale(g11, a1), dd_scale(g01, 2.0 * a0)), a1)
    t0 = dd_scale(dd_scale(g00, a0), a0)
    w2 = dd_add(dd_add(t2, t1), t0)
    n2 = jnp.sqrt(jnp.maximum(w2[0], 0.0) / (snf * snf) + norm_eps)
    k1 = 1.0 / snf
    k2 = 1.0 / (snf * n2)
    for i in range(3):
        v0, v1, v2 = v0_ref[i], v1_ref[i], v2_ref[i]
        basis_ref[0, i] = (v1 - p * v0) * k1
        basis_ref[1, i] = (v2 + a1 * v1 + a0 * v0) * k2
    top = jnp.concatenate([p, nf, none], axis=1)
    bottom = jnp.concatenate([pc, ps, n2], axis=1)
    hess_ref[...] = jnp.concatenate([top, bottom], axis=0)


def dd_div_const(hi, lo, size_all):
    d = jnp.full(hi.shape, float(size_all), f32)
    q = hi / d
    p, e = two_prod(q, d)
    rest = ((hi - p) - e) + lo
    return q, rest / d


def per_device(
    right_side, vertices, panels, near_owner, near_local, far_owner, far_local, far_left, far_right
):
    n = lax.axis_size("dev")
    clusters, _, width = right_side.shape
    near_count = near_owner.shape[0]
    far_count = far_owner.shape[0]
    cap = max(2, 4 * near_count // n)
    size_all = clusters * n * 3 * width
    x0 = right_side.transpose(1, 0, 2)
    shape = jax.ShapeDtypeStruct

    def exchange(block):
        return lax.all_to_all(block, "dev", split_axis=0, concat_axis=0, tiled=True)

    slots = max(128, 2 * cap)
    ask, idx = pl.pallas_call(
        lambda *refs: prep_kernel(*refs, cap=cap, trash=clusters),
        out_shape=(shape((n, slots), jnp.int32), shape((8, 2 * near_count), jnp.int32)),
        compiler_params=params(60),
        name="prep",
    )(near_owner.T, near_local.T, far_owner.T, far_local.T)
    asked = exchange(ask)

    rows3 = shape((n * 3 * cap, width), f32)
    both = shape((n * 6 * cap, width), f32)

    def flat(array):
        return array.reshape(-1, width)

    near_out = (
        pl.pallas_call(
            lambda *refs: pack_near_kernel(*refs, n=n, slots=cap),
            out_shape=shape((n * 6 * cap, width), f32),
            in_specs=[SM, VM, VM],
            scratch_shapes=[pltpu.VMEM((3 * clusters, width), f32)],
            compiler_params=params(60),
            cost_estimate=cost(4.0),
            name="pack_near",
        )(asked, flat(vertices.transpose(1, 0, 2)), flat(panels.transpose(1, 0, 2)))
    )
    near_in = exchange(near_out)
    x0_out = pl.pallas_call(
        lambda *refs: pack_kernel(*refs, n=n, slots=2 * cap),
        out_shape=both,
        in_specs=[SM, VM],
        compiler_params=params(),
        cost_estimate=cost(3.0),
        name="pack",
    )(asked, flat(x0))
    x0_in = exchange(x0_out)

    group = 8
    k_block = (group, 6, width, width)
    k_shape = shape((near_count, 6, width, width), f32)
    weight_shape = (n, cap, width)

    def whole(*dims):
        return pl.BlockSpec(dims, lambda g: (0,) * len(dims))

    def skews(comps):
        return [pltpu.VMEM((comps, 8, width), f32)] * 2 + [
            pltpu.VMEM((comps, width, width), f32)
        ] * 2

    stored, weights = pl.pallas_call(
        lambda *refs: build_kernel(*refs, cap=cap, count=near_count),
        out_shape=(k_shape, shape(weight_shape, f32)),
        grid=(near_count // group,),
        in_specs=[SM, whole(n, 6, cap, width)],
        out_specs=(pl.BlockSpec(k_block, lambda g: (g, 0, 0, 0)), whole(*weight_shape)),
        scratch_shapes=[pltpu.VMEM((n, 9 * cap, width), f32)] + skews(9),
        compiler_params=params(44),
        cost_estimate=cost(50.0),
        name="build",
    )(idx, near_in.reshape(n, 6, cap, width))

    def far_product(received):
        return pl.pallas_call(
            lambda *refs: far_kernel(*refs, cap=cap),
            out_shape=rows3,
            in_specs=[SM, VM, VM, VM],
            scratch_shapes=[
                pltpu.VMEM((far_count * 48, width), f32),
                pltpu.VMEM((6 * far_count, width), f32),
            ],
            compiler_params=params(8),
            cost_estimate=cost(5.0),
            name="far",
        )(idx, received, far_left, far_right)

    far_terms = far_product(x0_in)
    far_back = exchange(far_terms)

    def apply_stored(received):
        return (
            pl.pallas_call(
                lambda *refs: apply_kernel(*refs, cap=cap, count=near_count),
                out_shape=rows3,
                in_specs=[SM, VM, VM, pl.BlockSpec(memory_space=pl.ANY)],
                scratch_shapes=[pltpu.VMEM((near_count * 24, width), f32)] * 2
                + [pltpu.VMEM((6 * near_count, width), f32)]
                + [pltpu.VMEM((n, 3 * cap, width), f32)]
                + [pltpu.VMEM((4, 4, 6, width, width), f32), pltpu.SemaphoreType.DMA((4,))]
                + skews(3),
                compiler_params=params(44),
                cost_estimate=cost(18.0),
                name="apply",
            )(idx, weights, received.reshape(n, 3, 2 * cap, width), stored)
        )

    near_terms = apply_stored(x0_in)
    near_back = exchange(near_terms)

    accs = [pltpu.VMEM(((clusters + 1) * 8, width), f32)] * 4
    x1, x1_out = pl.pallas_call(
        lambda *refs: merge_kernel(*refs, n=n, cap=cap),
        out_shape=(shape((3, clusters, width), f32), both),
        in_specs=[SM, VM, VM],
        scratch_shapes=accs,
        compiler_params=params(),
        cost_estimate=cost(5.0),
        name="merge",
    )(asked, near_back, far_back)
    x1_in = exchange(x1_out)
    far_terms2 = far_product(x1_in)
    far_back2 = exchange(far_terms2)
    near_terms2 = apply_stored(x1_in)
    near_back2 = exchange(near_terms2)

    x2, part = pl.pallas_call(
        lambda *refs: gram_kernel(*refs, n=n, cap=cap),
        out_shape=(shape((3, clusters, width), f32), shape((n, 128), f32)),
        in_specs=[SM, VM, VM, VM, VM],
        scratch_shapes=accs,
        compiler_params=params(),
        cost_estimate=cost(5.0),
        name="gram",
    )(asked, near_back2, far_back2, x0, x1)
    parts = exchange(part)
    basis, hess = pl.pallas_call(
        lambda *refs: final_kernel(*refs, size_all=size_all),
        out_shape=(shape((2, 3, clusters, width), f32), shape((2, 3), f32)),
        compiler_params=params(),
        name="final",
    )(parts, x0, x1, x2)
    return (basis.transpose(0, 2, 1, 3), hess.T)


def solution(mesh):
    per_cluster = P("dev", None, None)
    per_pair = P("dev", None)
    in_specs = (per_cluster,) * 3 + (per_pair,) * 4 + (per_cluster,) * 2
    out_specs = (P(None, "dev", None, None), P())

    return jax.shard_map(
        per_device, mesh=mesh, in_specs=in_specs, out_specs=out_specs, check_vma=False
    )
```

```python
import jax
import jax.numpy as jnp
from jax import lax
from jax.experimental import pallas as pl
from jax.experimental.pallas import tpu as pltpu
from jax.sharding import PartitionSpec as P


soft_sq = 0.0025
area_floor = 6.25e-06
kelvin_diag = 1.8
norm_eps = 1e-06
big = 2.0 / 3.0
small = 1.0 / 6.0
BUILD_UNROLL = 16
APPLY_UNROLL = 16
f32 = jnp.float32
VM = pl.BlockSpec(memory_space=pltpu.VMEM)
SM = pl.BlockSpec(memory_space=pltpu.SMEM)


def params(mib=8):
    return pltpu.CompilerParams(vmem_limit_bytes=mib << 20)


def cost(us):
    return pl.CostEstimate(flops=0, transcendentals=0, bytes_accessed=int(us * 3.0e6))


def two_sum(a, b):
    s = a + b
    t = s - a
    return s, (a - (s - t)) + (b - t)


def split(a):
    c = a * 4097.0
    hi = c - (c - a)
    return hi, a - hi


def two_prod(a, b):
    p = a * b
    ah, al = split(a)
    bh, bl = split(b)
    return p, ((ah * bh - p) + ah * bl + al * bh) + al * bl


def dd_add(x, y):
    s, e = two_sum(x[0], y[0])
    e = e + (x[1] + y[1])
    hi = s + e
    return hi, e - (hi - s)


def dd_scale(x, f):
    p, e = two_prod(x[0], f)
    e = e + x[1] * f
    hi = p + e
    return hi, e - (hi - p)


def prep_kernel(no_ref, nl_ref, fo_ref, fl_ref, ask_ref, idx_ref, *, cap, trash):
    n = ask_ref.shape[0]
    width = 2 * no_ref.shape[1]
    ask = jnp.full(ask_ref.shape, float(trash), f32)
    rows = []
    for part, (o_ref, l_ref) in enumerate(((no_ref, nl_ref), (fo_ref, fl_ref))):
        owner = jnp.concatenate([o_ref[0:1, :], o_ref[1:2, :]], axis=1).astype(f32)
        local = jnp.concatenate([l_ref[0:1, :], l_ref[1:2, :]], axis=1).astype(f32)
        across = jnp.broadcast_to(owner, (width, width))
        down = across.T
        row = lax.broadcasted_iota(jnp.int32, (width, width), 0)
        col = lax.broadcasted_iota(jnp.int32, (width, width), 1)
        earlier = jnp.where((across == down) & (row < col), 1.0, 0.0)
        rank = jnp.sum(earlier, axis=0, keepdims=True)
        dest = lax.broadcasted_iota(jnp.int32, (n, width), 0).astype(f32)
        lhs = jnp.where(dest == owner, local + 1.0, 0.0).astype(jnp.bfloat16)
        slot = lax.broadcasted_iota(jnp.int32, (ask_ref.shape[1], width), 0).astype(f32)
        rhs = jnp.where(slot == rank + float(part * cap), 1.0, 0.0).astype(jnp.bfloat16)
        found = lax.dot_general(
            lhs, rhs, (((1,), (1,)), ((), ())), preferred_element_type=f32
        )
        ask = jnp.where(found > 0.5, found - 1.0, ask)
        rows += [owner, rank]
    ask_ref[...] = ask.astype(jnp.int32)
    idx_ref[...] = jnp.concatenate(rows + rows, axis=0).astype(jnp.int32)


def pack_rows(ask_ref, fetch, out_ref, *, n, slots, rows):
    def body(d, _):
        for s in range(slots):
            out_ref[pl.ds(d * rows * slots + s, rows, stride=slots), :] = fetch(ask_ref[d, s])
        return 0

    lax.fori_loop(0, n, body, 0, unroll=2)


def cluster_rows(ref, rows):
    clusters = ref.shape[0] // rows

    def fetch(c):
        return ref[pl.ds(jnp.minimum(c, clusters - 1), rows, stride=clusters), :]

    return fetch


def pack_kernel(ask_ref, x_ref, out_ref, *, n, slots):
    pack_rows(ask_ref, cluster_rows(x_ref, 3), out_ref, n=n, slots=slots, rows=3)


def pack_near_kernel(ask_ref, v_ref, p_ref, out_ref, all_ref, *, n, slots):
    half = v_ref.shape[0]
    all_ref[pl.ds(0, half), :] = v_ref[...]
    all_ref[pl.ds(half, half), :] = p_ref[...].astype(f32)
    pack_rows(ask_ref, cluster_rows(all_ref, 6), out_ref, n=n, slots=slots, rows=6)


def far_kernel(idx_ref, x_ref, l_ref, r_ref, out_ref, sum_ref, row_ref, *, cap):
    count = l_ref.shape[0]

    def ends(f):
        oa, ra = idx_ref[2, f], idx_ref[3, f]
        ob, rb = idx_ref[2, count + f], idx_ref[3, count + f]
        return (oa, ra), (ob, rb)

    def body(f, _):
        (oa, ra), (ob, rb) = ends(f)
        left = [l_ref[f, :, pl.ds(128 * i, 128)] for i in range(3)]
        right = [r_ref[f, :, pl.ds(128 * i, 128)] for i in range(3)]
        xa = [x_ref[pl.ds((oa * 3 + i) * 2 * cap + cap + ra, 1), :] for i in range(3)]
        xb = [x_ref[pl.ds((ob * 3 + i) * 2 * cap + cap + rb, 1), :] for i in range(3)]
        coef_b = jnp.sum(sum(right[i] * xb[i] for i in range(3)), axis=1, keepdims=True)
        coef_a = jnp.sum(sum(left[i] * xa[i] for i in range(3)), axis=1, keepdims=True)
        rank = left[0].shape[0]
        for i in range(3):
            for k, term in ((i, left[i] * coef_b), (3 + i, right[i] * coef_a)):
                at = pl.ds(pl.multiple_of((6 * f + k) * 8, 8), 8)
                sum_ref[at, :] = sum(term[8 * h : 8 * h + 8] for h in range(rank // 8))
        return 0

    lax.fori_loop(0, count, body, 0, unroll=8)

    def add_rows(q, _):
        for k in range(6):
            rows = [sum_ref[pl.ds(48 * 8 * q + 8 * k + m, 8, stride=48), :] for m in range(8)]
            row_ref[pl.ds(pl.multiple_of(k * count + 8 * q, 8), 8), :] = sum(rows)
        return 0

    lax.fori_loop(0, count // 8, add_rows, 0, unroll=2)

    def send(f, _):
        (oa, ra), (ob, rb) = ends(f)
        out_ref[pl.ds(oa * 3 * cap + ra, 3, stride=cap), :] = row_ref[pl.ds(f, 3, stride=count), :]
        out_ref[pl.ds(ob * 3 * cap + rb, 3, stride=cap), :] = row_ref[
            pl.ds(3 * count + f, 3, stride=count), :
        ]
        return 0

    lax.fori_loop(0, count, send, 0, unroll=8)


def slot_geometry(in_ref, geo_ref, w_ref, *, cap):
    n = in_ref.shape[0]

    def body(d, _):
        corner = []
        for m in range(3):
            pick = in_ref[d, 3 + m].astype(jnp.int32)
            corner.append(
                [jnp.take_along_axis(in_ref[d, i], pick, axis=1) for i in range(3)]
            )
        e1 = [corner[1][i] - corner[0][i] for i in range(3)]
        e2 = [corner[2][i] - corner[0][i] for i in range(3)]
        cx = e1[1] * e2[2] - e1[2] * e2[1]
        cy = e1[2] * e2[0] - e1[0] * e2[2]
        cz = e1[0] * e2[1] - e1[1] * e2[0]
        weight = jnp.sqrt(cx * cx + cy * cy + cz * cz + area_floor) / 6.0
        for s in range(3):
            for i in range(3):
                point = sum((big if m == s else small) * corner[m][i] for m in range(3))
                geo_ref[d, pl.ds((3 * s + i) * cap, cap), :] = point
        w_ref[d] = weight
        return 0

    lax.fori_loop(0, n, body, 0)


def pair_ends(idx_ref, pair, count):
    return (
        (idx_ref[0, pair], idx_ref[1, pair]),
        (idx_ref[0, count + pair], idx_ref[1, count + pair]),
    )


def skew_start(idx_ref, parts, base_ref, pair, *, cap, count):
    (oa, ra), _ = pair_ends(idx_ref, pair, count)
    at = 0
    for ref, comps in parts:
        for c in range(comps):
            row = jnp.broadcast_to(ref[oa, pl.ds(c * cap + ra, 1), :], (8, 128))
            base_ref[at + c] = pltpu.roll(row, 0, 1, stride=1, stride_axis=0)
        at += comps


def tile_rows(t):
    return pl.ds(8 * t if isinstance(t, int) else pl.multiple_of(8 * t, 8), 8)


def lane_roll(x, shift):
    return x if isinstance(shift, int) and shift == 0 else pltpu.roll(x, shift, 1)


def skew_tile(base_ref, dst_ref, t):
    for c in range(base_ref.shape[0]):
        dst_ref[c, tile_rows(t), :] = lane_roll(base_ref[c], 8 * t)


def weighted(w_ref, x_ref, y_ref, *, cap):
    def body(d, _):
        for i in range(3):
            y_ref[d, pl.ds(i * cap, cap), :] = w_ref[d] * x_ref[d, i, pl.ds(0, cap), :]
        return 0

    lax.fori_loop(0, x_ref.shape[0], body, 0, unroll=4)


def apply_tile(mats, ya, yb, second):
    kxx, kxy, kxz, kyy, kyz, kzz = mats
    full = ((kxx, kxy, kxz), (kxy, kyy, kyz), (kxz, kyz, kzz))
    firsts = [full[i][0] * yb[0] + full[i][1] * yb[1] + full[i][2] * yb[2] for i in range(3)]
    second = [
        second[j] + (full[0][j] * ya[0] + full[1][j] * ya[1] + full[2][j] * ya[2])
        for j in range(3)
    ]
    return firsts, second


def return_terms(idx_ref, w_ref, first_ref, second_ref, out_ref, row_ref, *, cap, count):
    def add_rows(q, _):
        for i in range(3):
            first = second = None
            for m in range(8):
                rows = pl.ds((24 * 8) * q + 8 * i + m, 8, stride=24)
                one, two = first_ref[rows, :], second_ref[rows, :]
                first = one if m == 0 else first + pltpu.roll(one, 128 - m, 1)
                second = two if m == 0 else second + two
            row_ref[pl.ds(pl.multiple_of(i * count + 8 * q, 8), 8), :] = first
            row_ref[pl.ds(pl.multiple_of((3 + i) * count + 8 * q, 8), 8), :] = second
        return 0

    lax.fori_loop(0, count // 8, add_rows, 0)

    def body(p, _):
        (oa, ra), (ob, rb) = pair_ends(idx_ref, p, count)
        wa = w_ref[oa, pl.ds(ra, 1), :]
        wb = w_ref[ob, pl.ds(rb, 1), :]
        first = row_ref[pl.ds(p, 3, stride=count), :]
        second = row_ref[pl.ds(3 * count + p, 3, stride=count), :]
        out_ref[pl.ds(oa * 3 * cap + ra, 3, stride=cap), :] = wa * first
        out_ref[pl.ds(ob * 3 * cap + rb, 3, stride=cap), :] = wb * second
        return 0

    lax.fori_loop(0, count, body, 0, unroll=8)


def near_tile(col, row):
    su = sv = xx = xy = xz = yy = yz = None
    for s in range(3):
        for q in range(3):
            x = col[3 * s] - row[3 * q]
            y = col[3 * s + 1] - row[3 * q + 1]
            z = col[3 * s + 2] - row[3 * q + 2]
            u = lax.rsqrt(x * x + y * y + z * z + soft_sq)
            v = u * u * u
            vx = v * x
            vy = v * y
            if su is None:
                su, sv = u, v
                xx, xy, xz, yy, yz = vx * x, vx * y, vx * z, vy * y, vy * z
            else:
                su, sv = su + u, sv + v
                xx, xy, xz = xx + vx * x, xy + vx * y, xz + vx * z
                yy, yz = yy + vy * y, yz + vy * z
    zz = su - soft_sq * sv - xx - yy
    diag = kelvin_diag * su
    return (xx + diag, xy, xz, yy + diag, yz, zz + diag)


def sweep_pairs(
    idx_ref, parts, bases, bufs, tile_mats, sums, *, step, pairs, group, cap, count, unroll, block
):
    def some_pairs(h, _):
        for j in range(block):
            src, dst, base = bufs[j % 2], bufs[1 - j % 2], bases[j % 2]
            g = block * h + j
            local = step * group + g
            pair = local
            following = jnp.minimum(pair + 1, pairs - 1)
            skew_start(idx_ref, parts, base, following, cap=cap, count=count)
            _, (ob, rb) = pair_ends(idx_ref, pair, count)
            row = [
                jnp.broadcast_to(ref[ob, pl.ds(c * cap + rb, 1), :], (8, 128))
                for ref, comps in parts
                for c in range(comps)
            ]
            comps = len(row)

            def tile_body(t, carry, g=g, src=src, dst=dst, base=base, row=row):
                if sums is not None:
                    held, first, second = carry
                    if not isinstance(t, int) or t > 0:
                        back = (128 - 8 * (t - 1)) % 128
                        first = [first[i] + lane_roll(held[i], back) for i in range(3)]
                skew_tile(base, dst, t)
                tile = tile_rows(t)
                col = [src[c, tile, :] for c in range(comps)]
                mats = tile_mats(g, tile, col, row)
                if sums is None:
                    return carry
                held, second = apply_tile(mats, col[comps - 3 :], row[comps - 3 :], second)
                return held, first, second

            zero = [jnp.zeros((8, 128), f32)] * 3
            start = 0 if sums is None else (zero, zero, zero)
            if unroll == 16:
                carry = start
                for t in range(16):
                    carry = tile_body(t, carry)
            else:
                carry = lax.fori_loop(0, 16, tile_body, start, unroll=unroll)
            if sums is not None:
                held, first, second = carry
                for i in range(3):
                    at = pl.ds(pl.multiple_of(24 * local + 8 * i, 8), 8)
                    sums[0][at, :] = first[i] + pltpu.roll(held[i], 8, 1)
                    sums[1][at, :] = second[i]
        return 0

    lax.fori_loop(0, group // block, some_pairs, 0)


def skew_first_pair(idx_ref, parts, base, buf, pair, *, cap, count):
    skew_start(idx_ref, parts, base, pair, cap=cap, count=count)

    def body(t, _):
        skew_tile(base, buf, t)
        return 0

    lax.fori_loop(0, 16, body, 0, unroll=4)


def build_kernel(idx_ref, in_ref, k_ref, w_ref, geo_ref, base0, base1, buf0, buf1, *, cap, count):
    step = pl.program_id(0)
    parts = ((geo_ref, 9),)

    @pl.when(step == 0)
    def _():
        slot_geometry(in_ref, geo_ref, w_ref, cap=cap)
        skew_first_pair(idx_ref, parts, base1, buf0, 0, cap=cap, count=count)

    def tile_mats(g, tile, col, row):
        mats = near_tile(col, row)
        for m in range(6):
            k_ref[g, m, tile, :] = mats[m]
        return mats

    sweep_pairs(
        idx_ref, parts, (base0, base1), (buf0, buf1), tile_mats, None,
        step=step, pairs=count, group=k_ref.shape[0], cap=cap, count=count,
        unroll=BUILD_UNROLL, block=4,
    )


def apply_kernel(
    idx_ref, w_ref, x_ref, k_hbm, out_ref,
    first_ref, second_ref, row_ref, y_ref, k_ref, sems, base0, base1, buf0, buf1, *, cap, count,
):
    depth, part = k_ref.shape[:2]
    groups = count // part
    parts = ((y_ref, 3),)

    def fetch(q, slot):
        return pltpu.make_async_copy(k_hbm.at[pl.ds(q * part, part)], k_ref.at[slot], sems.at[slot])

    for q in range(min(depth, groups)):
        fetch(q, q).start()
    weighted(w_ref, x_ref, y_ref, cap=cap)
    skew_first_pair(idx_ref, parts, base1, buf0, 0, cap=cap, count=count)

    def body(q, _):
        slot = lax.rem(q, depth)
        fetch(q, slot).wait()

        def tile_mats(g, tile, col, row):
            return [k_ref[slot, g, m, tile, :] for m in range(6)]

        sweep_pairs(
            idx_ref, parts, (base0, base1), (buf0, buf1), tile_mats, (first_ref, second_ref),
            step=q, pairs=count, group=part, cap=cap, count=count,
            unroll=APPLY_UNROLL, block=part,
        )

        @pl.when(q + depth < groups)
        def _():
            fetch(q + depth, slot).start()

        return 0

    lax.fori_loop(0, groups, body, 0)
    return_terms(idx_ref, w_ref, first_ref, second_ref, out_ref, row_ref, cap=cap, count=count)


def add_up(ask_ref, near_ref, far_ref, accs, out_ref, *, n, cap):
    clusters = out_ref.shape[1]
    for acc in accs:
        acc[...] = jnp.zeros(acc.shape, f32)

    def body(d, _):
        for s in range(cap):
            for part, ref in enumerate((near_ref, far_ref)):
                acc = accs[2 * part + s % 2]
                at = pl.ds(pl.multiple_of(8 * ask_ref[d, part * cap + s], 8), 3)
                acc[at, :] += ref[pl.ds(d * 3 * cap + s, 3, stride=cap), :]
        return 0

    lax.fori_loop(0, n, body, 0)

    def total(q, _):
        at = pl.ds(pl.multiple_of(64 * q, 64), 64)
        accs[0][at, :] = (accs[0][at, :] + accs[1][at, :]) + (accs[2][at, :] + accs[3][at, :])
        for i in range(3):
            out_ref[i, pl.ds(pl.multiple_of(8 * q, 8), 8), :] = accs[0][
                pl.ds(64 * q + i, 8, stride=8), :
            ]
        return 0

    lax.fori_loop(0, clusters // 8, total, 0)


def merge_kernel(ask_ref, rn_ref, rf_ref, out_ref, pack_ref, *accs, n, cap):
    add_up(ask_ref, rn_ref, rf_ref, accs, out_ref, n=n, cap=cap)
    last = out_ref.shape[1] - 1

    def fetch(c):
        return accs[0][pl.ds(pl.multiple_of(8 * jnp.minimum(c, last), 8), 3), :]

    pack_rows(ask_ref, fetch, pack_ref, n=n, slots=2 * cap, rows=3)


PRODUCTS = ((0, 0), (0, 1), (1, 1), (0, 2), (1, 2), (2, 2))


def gram_kernel(ask_ref, rn_ref, rf_ref, v0_ref, v1_ref, out_ref, part_ref, *accs, n, cap):
    add_up(ask_ref, rn_ref, rf_ref, accs, out_ref, n=n, cap=cap)
    clusters = out_ref.shape[1]
    refs = (v0_ref, v1_ref, out_ref)
    zero = jnp.zeros((8, 128), f32)
    totals = [(zero, zero)] * 6
    for i in range(3):

        def body(t, totals):
            tiles = [ref[i, pl.ds(8 * t, 8), :] for ref in refs]
            halves = [split(tile) for tile in tiles]
            new = []
            for k, (a, b) in enumerate(PRODUCTS):
                (ah, al), (bh, bl) = halves[a], halves[b]
                p = tiles[a] * tiles[b]
                e = ((ah * bh - p) + ah * bl + al * bh) + al * bl
                hi, lo = totals[k]
                s, err = two_sum(hi, p)
                new.append((s, lo + (err + e)))
            return new

        totals = lax.fori_loop(0, clusters // 8, body, totals)
    hi = jnp.concatenate([t[0] for t in totals], axis=0)
    lo = jnp.concatenate([t[1] for t in totals], axis=0)
    for shift in (64, 32, 16, 8, 4, 2, 1):
        hi, lo = dd_add((hi, lo), (pltpu.roll(hi, shift, 1), pltpu.roll(lo, shift, 1)))
    lane = lax.broadcasted_iota(jnp.int32, (8, 128), 1)
    shi = slo = zero
    for k in range(6):
        shi = jnp.where(lane == k, hi[8 * k : 8 * k + 8], shi)
        slo = jnp.where(lane == k, lo[8 * k : 8 * k + 8], slo)
    for shift in (4, 2, 1):
        shi, slo = dd_add((shi, slo), (pltpu.roll(shi, shift, 0), pltpu.roll(slo, shift, 0)))
    packed = jnp.where(lane < 8, shi, pltpu.roll(slo, 8, 1))
    part_ref[...] = jnp.broadcast_to(packed[0:1, :], part_ref.shape)


def final_kernel(part_ref, v0_ref, v1_ref, v2_ref, basis_ref, hess_ref, *, size_all):
    hi = part_ref[...]
    lo = pltpu.roll(hi, 120, 1)
    rows = hi.shape[0]
    while rows > 1:
        half = rows // 2
        hi, lo = dd_add((hi[:half], lo[:half]), (hi[half:], lo[half:]))
        rows = half
    inv = 1.0 / size_all
    hi, lo = dd_scale((hi, lo), jnp.full(hi.shape, inv, f32)) if size_all & (size_all - 1) == 0 else dd_div_const(hi, lo, size_all)
    g = [(hi[:, k : k + 1], lo[:, k : k + 1]) for k in range(6)]
    g00, g01, g11, g02, g12, g22 = g
    eps = jnp.full((1, 1), norm_eps, f32)
    none = jnp.zeros((1, 1), f32)
    s2 = dd_add(g00, (eps, none))
    s = jnp.sqrt(s2[0])
    p = g01[0] / s2[0]
    r1 = dd_add(g11, dd_scale(dd_add(dd_scale(g00, p), dd_scale(g01, none - 2.0)), p))
    nf = jnp.sqrt(jnp.maximum(r1[0], 0.0) / s2[0] + norm_eps)
    snf = s * nf
    c0 = dd_add(g02, dd_scale(g01, -p))
    pc = c0[0] / (s2[0] * nf)
    c1 = dd_add(dd_add(g12, dd_scale(g11, -p)), dd_scale(c0, -p))
    ps = c1[0] / (s2[0] * nf * nf)
    a1 = -(p + ps)
    a0 = ps * p - pc * nf
    t2 = dd_add(g22, dd_scale(dd_add(dd_scale(g12, a1), dd_scale(g02, a0)), none + 2.0))
    t1 = dd_scale(dd_add(dd_scale(g11, a1), dd_scale(g01, 2.0 * a0)), a1)
    t0 = dd_scale(dd_scale(g00, a0), a0)
    w2 = dd_add(dd_add(t2, t1), t0)
    n2 = jnp.sqrt(jnp.maximum(w2[0], 0.0) / (snf * snf) + norm_eps)
    k1 = 1.0 / snf
    k2 = 1.0 / (snf * n2)
    for i in range(3):
        v0, v1, v2 = v0_ref[i], v1_ref[i], v2_ref[i]
        basis_ref[0, i] = (v1 - p * v0) * k1
        basis_ref[1, i] = (v2 + a1 * v1 + a0 * v0) * k2
    top = jnp.concatenate([p, nf, none], axis=1)
    bottom = jnp.concatenate([pc, ps, n2], axis=1)
    hess_ref[...] = jnp.concatenate([top, bottom], axis=0)


def dd_div_const(hi, lo, size_all):
    d = jnp.full(hi.shape, float(size_all), f32)
    q = hi / d
    p, e = two_prod(q, d)
    rest = ((hi - p) - e) + lo
    return q, rest / d


def per_device(
    right_side, vertices, panels, near_owner, near_local, far_owner, far_local, far_left, far_right
):
    n = lax.axis_size("dev")
    clusters, _, width = right_side.shape
    near_count = near_owner.shape[0]
    far_count = far_owner.shape[0]
    cap = max(2, 4 * near_count // n)
    size_all = clusters * n * 3 * width
    x0 = right_side.transpose(1, 0, 2)
    shape = jax.ShapeDtypeStruct

    def exchange(block):
        return lax.all_to_all(block, "dev", split_axis=0, concat_axis=0, tiled=True)

    slots = max(128, 2 * cap)
    ask, idx = pl.pallas_call(
        lambda *refs: prep_kernel(*refs, cap=cap, trash=clusters),
        out_shape=(shape((n, slots), jnp.int32), shape((8, 2 * near_count), jnp.int32)),
        compiler_params=params(60),
        name="prep",
    )(near_owner.T, near_local.T, far_owner.T, far_local.T)
    asked = exchange(ask)

    rows3 = shape((n * 3 * cap, width), f32)
    both = shape((n * 6 * cap, width), f32)

    def flat(array):
        return array.reshape(-1, width)

    near_out = (
        pl.pallas_call(
            lambda *refs: pack_near_kernel(*refs, n=n, slots=cap),
            out_shape=shape((n * 6 * cap, width), f32),
            in_specs=[SM, VM, VM],
            scratch_shapes=[pltpu.VMEM((6 * clusters, width), f32)],
            compiler_params=params(60),
            cost_estimate=cost(4.0),
            name="pack_near",
        )(asked, flat(vertices.transpose(1, 0, 2)), flat(panels.transpose(1, 0, 2)))
    )
    near_in = exchange(near_out)
    x0_out = pl.pallas_call(
        lambda *refs: pack_kernel(*refs, n=n, slots=2 * cap),
        out_shape=both,
        in_specs=[SM, VM],
        compiler_params=params(),
        cost_estimate=cost(3.0),
        name="pack",
    )(asked, flat(x0))
    x0_in = exchange(x0_out)

    group = 8
    k_block = (group, 6, width, width)
    k_shape = shape((near_count, 6, width, width), f32)
    weight_shape = (n, cap, width)

    def whole(*dims):
        return pl.BlockSpec(dims, lambda g: (0,) * len(dims))

    def skews(comps):
        return [pltpu.VMEM((comps, 8, width), f32)] * 2 + [
            pltpu.VMEM((comps, width, width), f32)
        ] * 2

    stored, weights = pl.pallas_call(
        lambda *refs: build_kernel(*refs, cap=cap, count=near_count),
        out_shape=(k_shape, shape(weight_shape, f32)),
        grid=(near_count // group,),
        in_specs=[SM, whole(n, 6, cap, width)],
        out_specs=(pl.BlockSpec(k_block, lambda g: (g, 0, 0, 0)), whole(*weight_shape)),
        scratch_shapes=[pltpu.VMEM((n, 9 * cap, width), f32)] + skews(9),
        compiler_params=params(44),
        cost_estimate=cost(50.0),
        name="build",
    )(idx, near_in.reshape(n, 6, cap, width))

    def far_product(received):
        return pl.pallas_call(
            lambda *refs: far_kernel(*refs, cap=cap),
            out_shape=rows3,
            in_specs=[SM, VM, VM, VM],
            scratch_shapes=[
                pltpu.VMEM((far_count * 48, width), f32),
                pltpu.VMEM((6 * far_count, width), f32),
            ],
            compiler_params=params(8),
            cost_estimate=cost(5.0),
            name="far",
        )(idx, received, far_left, far_right)

    far_terms = far_product(x0_in)
    far_back = exchange(far_terms)

    def apply_stored(received):
        return (
            pl.pallas_call(
                lambda *refs: apply_kernel(*refs, cap=cap, count=near_count),
                out_shape=rows3,
                in_specs=[SM, VM, VM, pl.BlockSpec(memory_space=pl.ANY)],
                scratch_shapes=[pltpu.VMEM((near_count * 24, width), f32)] * 2
                + [pltpu.VMEM((6 * near_count, width), f32)]
                + [pltpu.VMEM((n, 3 * cap, width), f32)]
                + [pltpu.VMEM((4, 4, 6, width, width), f32), pltpu.SemaphoreType.DMA((4,))]
                + skews(3),
                compiler_params=params(44),
                cost_estimate=cost(18.0),
                name="apply",
            )(idx, weights, received.reshape(n, 3, 2 * cap, width), stored)
        )

    near_terms = apply_stored(x0_in)
    near_back = exchange(near_terms)

    accs = [pltpu.VMEM(((clusters + 1) * 8, width), f32)] * 4
    x1, x1_out = pl.pallas_call(
        lambda *refs: merge_kernel(*refs, n=n, cap=cap),
        out_shape=(shape((3, clusters, width), f32), both),
        in_specs=[SM, VM, VM],
        scratch_shapes=accs,
        compiler_params=params(),
        cost_estimate=cost(5.0),
        name="merge",
    )(asked, near_back, far_back)
    x1_in = exchange(x1_out)
    far_terms2 = far_product(x1_in)
    far_back2 = exchange(far_terms2)
    near_terms2 = apply_stored(x1_in)
    near_back2 = exchange(near_terms2)

    x2, part = pl.pallas_call(
        lambda *refs: gram_kernel(*refs, n=n, cap=cap),
        out_shape=(shape((3, clusters, width), f32), shape((n, 128), f32)),
        in_specs=[SM, VM, VM, VM, VM],
        scratch_shapes=accs,
        compiler_params=params(),
        cost_estimate=cost(5.0),
        name="gram",
    )(asked, near_back2, far_back2, x0, x1)
    parts = exchange(part)
    basis, hess = pl.pallas_call(
        lambda *refs: final_kernel(*refs, size_all=size_all),
        out_shape=(shape((2, 3, clusters, width), f32), shape((2, 3), f32)),
        compiler_params=params(),
        name="final",
    )(parts, x0, x1, x2)
    return (basis.transpose(0, 2, 1, 3), hess.T)


def solution(mesh):
    per_cluster = P("dev", None, None)
    per_pair = P("dev", None)
    in_specs = (per_cluster,) * 3 + (per_pair,) * 4 + (per_cluster,) * 2
    out_specs = (P(None, "dev", None, None), P())

    return jax.shard_map(
        per_device, mesh=mesh, in_specs=in_specs, out_specs=out_specs, check_vma=False
    )
```

```python
import jax
import jax.numpy as jnp
from jax import lax
from jax.experimental import pallas as pl
from jax.experimental.pallas import tpu as pltpu
from jax.sharding import PartitionSpec as P


soft_sq = 0.0025
area_floor = 6.25e-06
kelvin_diag = 1.8
norm_eps = 1e-06
big = 2.0 / 3.0
small = 1.0 / 6.0
BUILD_UNROLL = 16
APPLY_UNROLL = 16
f32 = jnp.float32
VM = pl.BlockSpec(memory_space=pltpu.VMEM)
SM = pl.BlockSpec(memory_space=pltpu.SMEM)


def params(mib=8):
    return pltpu.CompilerParams(vmem_limit_bytes=mib << 20)


def cost(us):
    return pl.CostEstimate(flops=0, transcendentals=0, bytes_accessed=int(us * 3.0e6))


def two_sum(a, b):
    s = a + b
    t = s - a
    return s, (a - (s - t)) + (b - t)


def split(a):
    c = a * 4097.0
    hi = c - (c - a)
    return hi, a - hi


def two_prod(a, b):
    p = a * b
    ah, al = split(a)
    bh, bl = split(b)
    return p, ((ah * bh - p) + ah * bl + al * bh) + al * bl


def dd_add(x, y):
    s, e = two_sum(x[0], y[0])
    e = e + (x[1] + y[1])
    hi = s + e
    return hi, e - (hi - s)


def dd_scale(x, f):
    p, e = two_prod(x[0], f)
    e = e + x[1] * f
    hi = p + e
    return hi, e - (hi - p)


def prep_kernel(no_ref, nl_ref, fo_ref, fl_ref, ask_ref, idx_ref, *, cap, trash):
    n = ask_ref.shape[0]
    width = 2 * no_ref.shape[1]
    ask = jnp.full(ask_ref.shape, float(trash), f32)
    rows = []
    for part, (o_ref, l_ref) in enumerate(((no_ref, nl_ref), (fo_ref, fl_ref))):
        owner = jnp.concatenate([o_ref[0:1, :], o_ref[1:2, :]], axis=1).astype(f32)
        local = jnp.concatenate([l_ref[0:1, :], l_ref[1:2, :]], axis=1).astype(f32)
        across = jnp.broadcast_to(owner, (width, width))
        down = across.T
        row = lax.broadcasted_iota(jnp.int32, (width, width), 0)
        col = lax.broadcasted_iota(jnp.int32, (width, width), 1)
        earlier = jnp.where((across == down) & (row < col), 1.0, 0.0)
        rank = jnp.sum(earlier, axis=0, keepdims=True)
        dest = lax.broadcasted_iota(jnp.int32, (n, width), 0).astype(f32)
        lhs = jnp.where(dest == owner, local + 1.0, 0.0).astype(jnp.bfloat16)
        slot = lax.broadcasted_iota(jnp.int32, (ask_ref.shape[1], width), 0).astype(f32)
        rhs = jnp.where(slot == rank + float(part * cap), 1.0, 0.0).astype(jnp.bfloat16)
        found = lax.dot_general(
            lhs, rhs, (((1,), (1,)), ((), ())), preferred_element_type=f32
        )
        ask = jnp.where(found > 0.5, found - 1.0, ask)
        rows += [owner, rank]
    ask_ref[...] = ask.astype(jnp.int32)
    idx_ref[...] = jnp.concatenate(rows + rows, axis=0).astype(jnp.int32)


def pack_rows(ask_ref, fetch, out_ref, *, n, slots, rows):
    def body(d, _):
        for s in range(slots):
            out_ref[pl.ds(d * rows * slots + s, rows, stride=slots), :] = fetch(ask_ref[d, s])
        return 0

    lax.fori_loop(0, n, body, 0, unroll=2)


def cluster_rows(ref, rows):
    clusters = ref.shape[0] // rows

    def fetch(c):
        return ref[pl.ds(jnp.minimum(c, clusters - 1), rows, stride=clusters), :]

    return fetch


def pack_kernel(ask_ref, x_ref, out_ref, *, n, slots):
    pack_rows(ask_ref, cluster_rows(x_ref, 3), out_ref, n=n, slots=slots, rows=3)


def pack_near_kernel(ask_ref, v_ref, p_ref, out_ref, all_ref, *, n, slots):
    half = v_ref.shape[0]
    all_ref[pl.ds(0, half), :] = v_ref[...]
    all_ref[pl.ds(half, half), :] = p_ref[...].astype(f32)
    pack_rows(ask_ref, cluster_rows(all_ref, 6), out_ref, n=n, slots=slots, rows=6)


def far_kernel(idx_ref, x_ref, l_ref, r_ref, out_ref, sum_ref, row_ref, *, cap):
    count = l_ref.shape[0]

    def ends(f):
        oa, ra = idx_ref[2, f], idx_ref[3, f]
        ob, rb = idx_ref[2, count + f], idx_ref[3, count + f]
        return (oa, ra), (ob, rb)

    def body(f, _):
        (oa, ra), (ob, rb) = ends(f)
        left = [l_ref[f, :, pl.ds(128 * i, 128)] for i in range(3)]
        right = [r_ref[f, :, pl.ds(128 * i, 128)] for i in range(3)]
        xa = [x_ref[pl.ds((oa * 3 + i) * 2 * cap + cap + ra, 1), :] for i in range(3)]
        xb = [x_ref[pl.ds((ob * 3 + i) * 2 * cap + cap + rb, 1), :] for i in range(3)]
        coef_b = jnp.sum(sum(right[i] * xb[i] for i in range(3)), axis=1, keepdims=True)
        coef_a = jnp.sum(sum(left[i] * xa[i] for i in range(3)), axis=1, keepdims=True)
        rank = left[0].shape[0]
        for i in range(3):
            for k, term in ((i, left[i] * coef_b), (3 + i, right[i] * coef_a)):
                at = pl.ds(pl.multiple_of((6 * f + k) * 8, 8), 8)
                sum_ref[at, :] = sum(term[8 * h : 8 * h + 8] for h in range(rank // 8))
        return 0

    lax.fori_loop(0, count, body, 0, unroll=8)

    def add_rows(q, _):
        for k in range(6):
            rows = [sum_ref[pl.ds(48 * 8 * q + 8 * k + m, 8, stride=48), :] for m in range(8)]
            row_ref[pl.ds(pl.multiple_of(k * count + 8 * q, 8), 8), :] = sum(rows)
        return 0

    lax.fori_loop(0, count // 8, add_rows, 0, unroll=2)

    def send(f, _):
        (oa, ra), (ob, rb) = ends(f)
        out_ref[pl.ds(oa * 3 * cap + ra, 3, stride=cap), :] = row_ref[pl.ds(f, 3, stride=count), :]
        out_ref[pl.ds(ob * 3 * cap + rb, 3, stride=cap), :] = row_ref[
            pl.ds(3 * count + f, 3, stride=count), :
        ]
        return 0

    lax.fori_loop(0, count, send, 0, unroll=8)


def slot_geometry(in_ref, geo_ref, w_ref, *, cap):
    n = in_ref.shape[0]

    def body(d, _):
        corner = []
        for m in range(3):
            pick = in_ref[d, 3 + m].astype(jnp.int32)
            corner.append(
                [jnp.take_along_axis(in_ref[d, i], pick, axis=1) for i in range(3)]
            )
        e1 = [corner[1][i] - corner[0][i] for i in range(3)]
        e2 = [corner[2][i] - corner[0][i] for i in range(3)]
        cx = e1[1] * e2[2] - e1[2] * e2[1]
        cy = e1[2] * e2[0] - e1[0] * e2[2]
        cz = e1[0] * e2[1] - e1[1] * e2[0]
        weight = jnp.sqrt(cx * cx + cy * cy + cz * cz + area_floor) / 6.0
        for s in range(3):
            for i in range(3):
                point = sum((big if m == s else small) * corner[m][i] for m in range(3))
                geo_ref[d, pl.ds((3 * s + i) * cap, cap), :] = point
        w_ref[d] = weight
        return 0

    lax.fori_loop(0, n, body, 0)


def pair_ends(idx_ref, pair, count):
    return (
        (idx_ref[0, pair], idx_ref[1, pair]),
        (idx_ref[0, count + pair], idx_ref[1, count + pair]),
    )


def skew_start(idx_ref, parts, base_ref, pair, *, cap, count):
    (oa, ra), _ = pair_ends(idx_ref, pair, count)
    at = 0
    for ref, comps in parts:
        for c in range(comps):
            row = jnp.broadcast_to(ref[oa, pl.ds(c * cap + ra, 1), :], (8, 128))
            base_ref[at + c] = pltpu.roll(row, 0, 1, stride=1, stride_axis=0)
        at += comps


def tile_rows(t):
    return pl.ds(8 * t if isinstance(t, int) else pl.multiple_of(8 * t, 8), 8)


def lane_roll(x, shift):
    return x if isinstance(shift, int) and shift == 0 else pltpu.roll(x, shift, 1)


def skew_tile(base_ref, dst_ref, t):
    for c in range(base_ref.shape[0]):
        dst_ref[c, tile_rows(t), :] = lane_roll(base_ref[c], 8 * t)


def weighted(w_ref, x_ref, y_ref, *, cap):
    def body(d, _):
        for i in range(3):
            y_ref[d, pl.ds(i * cap, cap), :] = w_ref[d] * x_ref[d, i, pl.ds(0, cap), :]
        return 0

    lax.fori_loop(0, x_ref.shape[0], body, 0, unroll=4)


def apply_tile(mats, ya, yb, second):
    kxx, kxy, kxz, kyy, kyz, kzz = mats
    full = ((kxx, kxy, kxz), (kxy, kyy, kyz), (kxz, kyz, kzz))
    firsts = [full[i][0] * yb[0] + full[i][1] * yb[1] + full[i][2] * yb[2] for i in range(3)]
    second = [
        second[j] + (full[0][j] * ya[0] + full[1][j] * ya[1] + full[2][j] * ya[2])
        for j in range(3)
    ]
    return firsts, second


def return_terms(idx_ref, w_ref, first_ref, second_ref, out_ref, row_ref, *, cap, count):
    def add_rows(q, _):
        for i in range(3):
            first = second = None
            for m in range(8):
                rows = pl.ds((24 * 8) * q + 8 * i + m, 8, stride=24)
                one, two = first_ref[rows, :], second_ref[rows, :]
                first = one if m == 0 else first + pltpu.roll(one, 128 - m, 1)
                second = two if m == 0 else second + two
            row_ref[pl.ds(pl.multiple_of(i * count + 8 * q, 8), 8), :] = first
            row_ref[pl.ds(pl.multiple_of((3 + i) * count + 8 * q, 8), 8), :] = second
        return 0

    lax.fori_loop(0, count // 8, add_rows, 0)

    def body(p, _):
        (oa, ra), (ob, rb) = pair_ends(idx_ref, p, count)
        wa = w_ref[oa, pl.ds(ra, 1), :]
        wb = w_ref[ob, pl.ds(rb, 1), :]
        first = row_ref[pl.ds(p, 3, stride=count), :]
        second = row_ref[pl.ds(3 * count + p, 3, stride=count), :]
        out_ref[pl.ds(oa * 3 * cap + ra, 3, stride=cap), :] = wa * first
        out_ref[pl.ds(ob * 3 * cap + rb, 3, stride=cap), :] = wb * second
        return 0

    lax.fori_loop(0, count, body, 0, unroll=8)


def near_tile(col, row):
    su = sv = xx = xy = xz = yy = yz = None
    for s in range(3):
        for q in range(3):
            x = col[3 * s] - row[3 * q]
            y = col[3 * s + 1] - row[3 * q + 1]
            z = col[3 * s + 2] - row[3 * q + 2]
            u = lax.rsqrt(x * x + y * y + z * z + soft_sq)
            v = u * u * u
            vx = v * x
            vy = v * y
            if su is None:
                su, sv = u, v
                xx, xy, xz, yy, yz = vx * x, vx * y, vx * z, vy * y, vy * z
            else:
                su, sv = su + u, sv + v
                xx, xy, xz = xx + vx * x, xy + vx * y, xz + vx * z
                yy, yz = yy + vy * y, yz + vy * z
    zz = su - soft_sq * sv - xx - yy
    diag = kelvin_diag * su
    return (xx + diag, xy, xz, yy + diag, yz, zz + diag)


def sweep_pairs(
    idx_ref, parts, bases, bufs, tile_mats, sums, *, step, pairs, group, cap, count, unroll, block
):
    def some_pairs(h, _):
        for j in range(block):
            src, dst, base = bufs[j % 2], bufs[1 - j % 2], bases[j % 2]
            g = block * h + j
            local = step * group + g
            pair = local
            following = jnp.minimum(pair + 1, pairs - 1)
            skew_start(idx_ref, parts, base, following, cap=cap, count=count)
            _, (ob, rb) = pair_ends(idx_ref, pair, count)
            row = [
                jnp.broadcast_to(ref[ob, pl.ds(c * cap + rb, 1), :], (8, 128))
                for ref, comps in parts
                for c in range(comps)
            ]
            comps = len(row)

            def tile_body(t, carry, g=g, src=src, dst=dst, base=base, row=row):
                if sums is not None:
                    held, first, second = carry
                    if not isinstance(t, int) or t > 0:
                        back = (128 - 8 * (t - 1)) % 128
                        first = [first[i] + lane_roll(held[i], back) for i in range(3)]
                skew_tile(base, dst, t)
                tile = tile_rows(t)
                col = [src[c, tile, :] for c in range(comps)]
                mats = tile_mats(g, tile, col, row)
                if sums is None:
                    return carry
                held, second = apply_tile(mats, col[comps - 3 :], row[comps - 3 :], second)
                return held, first, second

            zero = [jnp.zeros((8, 128), f32)] * 3
            start = 0 if sums is None else (zero, zero, zero)
            if unroll == 16:
                carry = start
                for t in range(16):
                    carry = tile_body(t, carry)
            else:
                carry = lax.fori_loop(0, 16, tile_body, start, unroll=unroll)
            if sums is not None:
                held, first, second = carry
                for i in range(3):
                    at = pl.ds(pl.multiple_of(24 * local + 8 * i, 8), 8)
                    sums[0][at, :] = first[i] + pltpu.roll(held[i], 8, 1)
                    sums[1][at, :] = second[i]
        return 0

    lax.fori_loop(0, group // block, some_pairs, 0)


def skew_first_pair(idx_ref, parts, base, buf, pair, *, cap, count):
    skew_start(idx_ref, parts, base, pair, cap=cap, count=count)

    def body(t, _):
        skew_tile(base, buf, t)
        return 0

    lax.fori_loop(0, 16, body, 0, unroll=4)


def build_kernel(idx_ref, in_ref, k_ref, w_ref, geo_ref, base0, base1, buf0, buf1, *, cap, count):
    step = pl.program_id(0)
    parts = ((geo_ref, 9),)

    @pl.when(step == 0)
    def _():
        slot_geometry(in_ref, geo_ref, w_ref, cap=cap)
        skew_first_pair(idx_ref, parts, base1, buf0, 0, cap=cap, count=count)

    def tile_mats(g, tile, col, row):
        mats = near_tile(col, row)
        for m in range(6):
            k_ref[g, m, tile, :] = mats[m]
        return mats

    sweep_pairs(
        idx_ref, parts, (base0, base1), (buf0, buf1), tile_mats, None,
        step=step, pairs=count, group=k_ref.shape[0], cap=cap, count=count,
        unroll=BUILD_UNROLL, block=8,
    )


def apply_kernel(
    idx_ref, w_ref, x_ref, k_hbm, out_ref,
    first_ref, second_ref, row_ref, y_ref, k_ref, sems, base0, base1, buf0, buf1, *, cap, count,
):
    depth, part = k_ref.shape[:2]
    groups = count // part
    parts = ((y_ref, 3),)

    def fetch(q, slot):
        return pltpu.make_async_copy(k_hbm.at[pl.ds(q * part, part)], k_ref.at[slot], sems.at[slot])

    for q in range(min(depth, groups)):
        fetch(q, q).start()
    weighted(w_ref, x_ref, y_ref, cap=cap)
    skew_first_pair(idx_ref, parts, base1, buf0, 0, cap=cap, count=count)

    def body(q, _):
        slot = lax.rem(q, depth)
        fetch(q, slot).wait()

        def tile_mats(g, tile, col, row):
            return [k_ref[slot, g, m, tile, :] for m in range(6)]

        sweep_pairs(
            idx_ref, parts, (base0, base1), (buf0, buf1), tile_mats, (first_ref, second_ref),
            step=q, pairs=count, group=part, cap=cap, count=count,
            unroll=APPLY_UNROLL, block=part,
        )

        @pl.when(q + depth < groups)
        def _():
            fetch(q + depth, slot).start()

        return 0

    lax.fori_loop(0, groups, body, 0)
    return_terms(idx_ref, w_ref, first_ref, second_ref, out_ref, row_ref, cap=cap, count=count)


def add_up(ask_ref, near_ref, far_ref, accs, out_ref, *, n, cap):
    clusters = out_ref.shape[1]
    for acc in accs:
        acc[...] = jnp.zeros(acc.shape, f32)

    def body(d, _):
        for s in range(cap):
            for part, ref in enumerate((near_ref, far_ref)):
                acc = accs[2 * part + s % 2]
                at = pl.ds(pl.multiple_of(8 * ask_ref[d, part * cap + s], 8), 3)
                acc[at, :] += ref[pl.ds(d * 3 * cap + s, 3, stride=cap), :]
        return 0

    lax.fori_loop(0, n, body, 0, unroll=4)

    def total(q, _):
        at = pl.ds(pl.multiple_of(64 * q, 64), 64)
        accs[0][at, :] = (accs[0][at, :] + accs[1][at, :]) + (accs[2][at, :] + accs[3][at, :])
        for i in range(3):
            out_ref[i, pl.ds(pl.multiple_of(8 * q, 8), 8), :] = accs[0][
                pl.ds(64 * q + i, 8, stride=8), :
            ]
        return 0

    lax.fori_loop(0, clusters // 8, total, 0, unroll=2)


def merge_kernel(ask_ref, rn_ref, rf_ref, out_ref, pack_ref, *accs, n, cap):
    add_up(ask_ref, rn_ref, rf_ref, accs, out_ref, n=n, cap=cap)
    last = out_ref.shape[1] - 1

    def fetch(c):
        return accs[0][pl.ds(pl.multiple_of(8 * jnp.minimum(c, last), 8), 3), :]

    pack_rows(ask_ref, fetch, pack_ref, n=n, slots=2 * cap, rows=3)


PRODUCTS = ((0, 0), (0, 1), (1, 1), (0, 2), (1, 2), (2, 2))


def gram_kernel(ask_ref, rn_ref, rf_ref, v0_ref, v1_ref, out_ref, part_ref, *accs, n, cap):
    add_up(ask_ref, rn_ref, rf_ref, accs, out_ref, n=n, cap=cap)
    clusters = out_ref.shape[1]
    refs = (v0_ref, v1_ref, out_ref)
    zero = jnp.zeros((8, 128), f32)
    totals = [(zero, zero)] * 6
    for i in range(3):

        def body(t, totals):
            tiles = [ref[i, pl.ds(8 * t, 8), :] for ref in refs]
            halves = [split(tile) for tile in tiles]
            new = []
            for k, (a, b) in enumerate(PRODUCTS):
                (ah, al), (bh, bl) = halves[a], halves[b]
                p = tiles[a] * tiles[b]
                e = ((ah * bh - p) + ah * bl + al * bh) + al * bl
                hi, lo = totals[k]
                s, err = two_sum(hi, p)
                new.append((s, lo + (err + e)))
            return new

        totals = lax.fori_loop(0, clusters // 8, body, totals, unroll=2)
    hi = jnp.concatenate([t[0] for t in totals], axis=0)
    lo = jnp.concatenate([t[1] for t in totals], axis=0)
    for shift in (64, 32, 16, 8, 4, 2, 1):
        hi, lo = dd_add((hi, lo), (pltpu.roll(hi, shift, 1), pltpu.roll(lo, shift, 1)))
    lane = lax.broadcasted_iota(jnp.int32, (8, 128), 1)
    shi = slo = zero
    for k in range(6):
        shi = jnp.where(lane == k, hi[8 * k : 8 * k + 8], shi)
        slo = jnp.where(lane == k, lo[8 * k : 8 * k + 8], slo)
    for shift in (4, 2, 1):
        shi, slo = dd_add((shi, slo), (pltpu.roll(shi, shift, 0), pltpu.roll(slo, shift, 0)))
    packed = jnp.where(lane < 8, shi, pltpu.roll(slo, 8, 1))
    part_ref[...] = jnp.broadcast_to(packed[0:1, :], part_ref.shape)


def final_kernel(part_ref, v0_ref, v1_ref, v2_ref, basis_ref, hess_ref, *, size_all):
    hi = part_ref[...]
    lo = pltpu.roll(hi, 120, 1)
    rows = hi.shape[0]
    while rows > 1:
        half = rows // 2
        hi, lo = dd_add((hi[:half], lo[:half]), (hi[half:], lo[half:]))
        rows = half
    inv = 1.0 / size_all
    hi, lo = dd_scale((hi, lo), jnp.full(hi.shape, inv, f32)) if size_all & (size_all - 1) == 0 else dd_div_const(hi, lo, size_all)
    g = [(hi[:, k : k + 1], lo[:, k : k + 1]) for k in range(6)]
    g00, g01, g11, g02, g12, g22 = g
    eps = jnp.full((1, 1), norm_eps, f32)
    none = jnp.zeros((1, 1), f32)
    s2 = dd_add(g00, (eps, none))
    s = jnp.sqrt(s2[0])
    p = g01[0] / s2[0]
    r1 = dd_add(g11, dd_scale(dd_add(dd_scale(g00, p), dd_scale(g01, none - 2.0)), p))
    nf = jnp.sqrt(jnp.maximum(r1[0], 0.0) / s2[0] + norm_eps)
    snf = s * nf
    c0 = dd_add(g02, dd_scale(g01, -p))
    pc = c0[0] / (s2[0] * nf)
    c1 = dd_add(dd_add(g12, dd_scale(g11, -p)), dd_scale(c0, -p))
    ps = c1[0] / (s2[0] * nf * nf)
    a1 = -(p + ps)
    a0 = ps * p - pc * nf
    t2 = dd_add(g22, dd_scale(dd_add(dd_scale(g12, a1), dd_scale(g02, a0)), none + 2.0))
    t1 = dd_scale(dd_add(dd_scale(g11, a1), dd_scale(g01, 2.0 * a0)), a1)
    t0 = dd_scale(dd_scale(g00, a0), a0)
    w2 = dd_add(dd_add(t2, t1), t0)
    n2 = jnp.sqrt(jnp.maximum(w2[0], 0.0) / (snf * snf) + norm_eps)
    k1 = 1.0 / snf
    k2 = 1.0 / (snf * n2)
    for i in range(3):
        v0, v1, v2 = v0_ref[i], v1_ref[i], v2_ref[i]
        basis_ref[0, i] = (v1 - p * v0) * k1
        basis_ref[1, i] = (v2 + a1 * v1 + a0 * v0) * k2
    top = jnp.concatenate([p, nf, none], axis=1)
    bottom = jnp.concatenate([pc, ps, n2], axis=1)
    hess_ref[...] = jnp.concatenate([top, bottom], axis=0)


def dd_div_const(hi, lo, size_all):
    d = jnp.full(hi.shape, float(size_all), f32)
    q = hi / d
    p, e = two_prod(q, d)
    rest = ((hi - p) - e) + lo
    return q, rest / d


def per_device(
    right_side, vertices, panels, near_owner, near_local, far_owner, far_local, far_left, far_right
):
    n = lax.axis_size("dev")
    clusters, _, width = right_side.shape
    near_count = near_owner.shape[0]
    far_count = far_owner.shape[0]
    cap = max(2, 4 * near_count // n)
    size_all = clusters * n * 3 * width
    x0 = right_side.transpose(1, 0, 2)
    shape = jax.ShapeDtypeStruct

    def exchange(block):
        return lax.all_to_all(block, "dev", split_axis=0, concat_axis=0, tiled=True)

    slots = max(128, 2 * cap)
    ask, idx = pl.pallas_call(
        lambda *refs: prep_kernel(*refs, cap=cap, trash=clusters),
        out_shape=(shape((n, slots), jnp.int32), shape((8, 2 * near_count), jnp.int32)),
        compiler_params=params(60),
        name="prep",
    )(near_owner.T, near_local.T, far_owner.T, far_local.T)
    asked = exchange(ask)

    rows3 = shape((n * 3 * cap, width), f32)
    both = shape((n * 6 * cap, width), f32)

    def flat(array):
        return array.reshape(-1, width)

    near_out = (
        pl.pallas_call(
            lambda *refs: pack_near_kernel(*refs, n=n, slots=cap),
            out_shape=shape((n * 6 * cap, width), f32),
            in_specs=[SM, VM, VM],
            scratch_shapes=[pltpu.VMEM((6 * clusters, width), f32)],
            compiler_params=params(60),
            cost_estimate=cost(4.0),
            name="pack_near",
        )(asked, flat(vertices.transpose(1, 0, 2)), flat(panels.transpose(1, 0, 2)))
    )
    near_in = exchange(near_out)
    x0_out = pl.pallas_call(
        lambda *refs: pack_kernel(*refs, n=n, slots=2 * cap),
        out_shape=both,
        in_specs=[SM, VM],
        compiler_params=params(),
        cost_estimate=cost(3.0),
        name="pack",
    )(asked, flat(x0))
    x0_in = exchange(x0_out)

    group = 8
    k_block = (group, 6, width, width)
    k_shape = shape((near_count, 6, width, width), f32)
    weight_shape = (n, cap, width)

    def whole(*dims):
        return pl.BlockSpec(dims, lambda g: (0,) * len(dims))

    def skews(comps):
        return [pltpu.VMEM((comps, 8, width), f32)] * 2 + [
            pltpu.VMEM((comps, width, width), f32)
        ] * 2

    stored, weights = pl.pallas_call(
        lambda *refs: build_kernel(*refs, cap=cap, count=near_count),
        out_shape=(k_shape, shape(weight_shape, f32)),
        grid=(near_count // group,),
        in_specs=[SM, whole(n, 6, cap, width)],
        out_specs=(pl.BlockSpec(k_block, lambda g: (g, 0, 0, 0)), whole(*weight_shape)),
        scratch_shapes=[pltpu.VMEM((n, 9 * cap, width), f32)] + skews(9),
        compiler_params=params(44),
        cost_estimate=cost(50.0),
        name="build",
    )(idx, near_in.reshape(n, 6, cap, width))

    def far_product(received):
        return pl.pallas_call(
            lambda *refs: far_kernel(*refs, cap=cap),
            out_shape=rows3,
            in_specs=[SM, VM, VM, VM],
            scratch_shapes=[
                pltpu.VMEM((far_count * 48, width), f32),
                pltpu.VMEM((6 * far_count, width), f32),
            ],
            compiler_params=params(8),
            cost_estimate=cost(5.0),
            name="far",
        )(idx, received, far_left, far_right)

    far_terms = far_product(x0_in)
    far_back = exchange(far_terms)

    def apply_stored(received):
        return (
            pl.pallas_call(
                lambda *refs: apply_kernel(*refs, cap=cap, count=near_count),
                out_shape=rows3,
                in_specs=[SM, VM, VM, pl.BlockSpec(memory_space=pl.ANY)],
                scratch_shapes=[pltpu.VMEM((near_count * 24, width), f32)] * 2
                + [pltpu.VMEM((6 * near_count, width), f32)]
                + [pltpu.VMEM((n, 3 * cap, width), f32)]
                + [pltpu.VMEM((4, 4, 6, width, width), f32), pltpu.SemaphoreType.DMA((4,))]
                + skews(3),
                compiler_params=params(44),
                cost_estimate=cost(18.0),
                name="apply",
            )(idx, weights, received.reshape(n, 3, 2 * cap, width), stored)
        )

    near_terms = apply_stored(x0_in)
    near_back = exchange(near_terms)

    accs = [pltpu.VMEM(((clusters + 1) * 8, width), f32)] * 4
    x1, x1_out = pl.pallas_call(
        lambda *refs: merge_kernel(*refs, n=n, cap=cap),
        out_shape=(shape((3, clusters, width), f32), both),
        in_specs=[SM, VM, VM],
        scratch_shapes=accs,
        compiler_params=params(),
        cost_estimate=cost(5.0),
        name="merge",
    )(asked, near_back, far_back)
    x1_in = exchange(x1_out)
    far_terms2 = far_product(x1_in)
    far_back2 = exchange(far_terms2)
    near_terms2 = apply_stored(x1_in)
    near_back2 = exchange(near_terms2)

    x2, part = pl.pallas_call(
        lambda *refs: gram_kernel(*refs, n=n, cap=cap),
        out_shape=(shape((3, clusters, width), f32), shape((n, 128), f32)),
        in_specs=[SM, VM, VM, VM, VM],
        scratch_shapes=accs,
        compiler_params=params(),
        cost_estimate=cost(5.0),
        name="gram",
    )(asked, near_back2, far_back2, x0, x1)
    parts = exchange(part)
    basis, hess = pl.pallas_call(
        lambda *refs: final_kernel(*refs, size_all=size_all),
        out_shape=(shape((2, 3, clusters, width), f32), shape((2, 3), f32)),
        compiler_params=params(),
        name="final",
    )(parts, x0, x1, x2)
    return (basis.transpose(0, 2, 1, 3), hess.T)


def solution(mesh):
    per_cluster = P("dev", None, None)
    per_pair = P("dev", None)
    in_specs = (per_cluster,) * 3 + (per_pair,) * 4 + (per_cluster,) * 2
    out_specs = (P(None, "dev", None, None), P())

    return jax.shard_map(
        per_device, mesh=mesh, in_specs=in_specs, out_specs=out_specs, check_vma=False
    )
```
